256 devices in a mesh: gz: 8 (over z), gy: 8 (over x, core), gx: 4 (over y).
Axes of the slice: x: 4, y: 4, z: 8, core: 2. Of those that a mesh axis runs over, the one named last changes fastest.
Arguments:
- fields: float32 [5, 256, 128, 512], P(None, 'gz', 'gy', 'gx'), may hold values from -6 to 6
- diffusivity: float32 [256, 128, 512], P('gz', 'gy', 'gx'), may hold values from 0.01 to 0.08
- courant: float32 [5, 3], replicated, may hold values from 0.03 to 0.1
- tf_center: float32 [16], replicated, may hold values from -1.5 to 1.5
- tf_sharp: float32 [16], replicated, may hold values from 0.5 to 4
- tf_gain: float32 [16], replicated, may hold values from 0.01 to 0.12
- tf_color: float32 [3, 16], replicated, may hold values from 0.2 to 1
- tile_mask: int32 [8, 16, 128, 4], P('gz', None, 'gy', 'gx'), may hold values from 0 to 1, as said below
- tile_perm: int32 [8, 4, 256], P('gy', 'gx'), may hold values from 0 to 255, each once within a row
Outputs:
- advanced: float32 [5, 256, 128, 512], P(None, 'gz', 'gy', 'gx')
- picture: float32 [8, 4, 256, 4, 128], P('gy', 'gx', 'gz')
The draws below stay inside these ranges and needn't reach their ends.
Inputs may be any that keep to these rules, and one draw needn't show every extreme that they name: `tile_mask`: 1 marks an active tile; the share of active tiles differs from slab to slab.
All inputs are finite; a program needn't handle non-finite values.
Results may differ from the reference program's by a relative error of at most 0.0001.
Values sent between devices are 32-bit elements; how exact they have to be, the bound alone decides.
A program may use at most 64 MiB of HBM per device.

```python
import math
import jax
import jax.numpy as jnp
from jax import lax

F = 5
TF = 16
CX = 128
CY = 16
CZ = 32
SLABS = 8
NZ = 256
NY = 128
NX = 512
NBY = 8
NBX = 4
TILES = 256


def draw_tile_mask(key, part):
    key_rate, key_roll = jax.random.split(jax.random.fold_in(key, 17))
    thresholds = jax.random.randint(key_rate, (SLABS, 1, 1, 1), 20, 96)
    rolls = jax.random.randint(key_roll, (SLABS, TF, NY, NX // 128), 0, 100)
    return (rolls < thresholds).astype(jnp.int32)


def levels(key, dims, cuts, least, high):
    level = 1.0
    for dim, parts in cuts:
        heights = jax.random.uniform(jax.random.fold_in(jax.random.fold_in(key, 6), dim), (parts,), jnp.float32, least / len(cuts), high / len(cuts))
        level = level * jnp.repeat(jnp.exp(heights), dims[dim] // parts).reshape((-1,) + (1,) * (len(dims) - 1 - dim))
    return level


def normal_values(rng, dims, spread, bound, cuts=(), dtype=jnp.bfloat16):
    level = levels(rng, dims, cuts, -0.22, 0.18) if cuts else 1.0
    drawn = jax.random.normal(rng, dims, jnp.float32) * spread * level
    return jnp.minimum(jnp.maximum(drawn, -bound), bound).astype(dtype)


def setup_inputs(seed: int = 0) -> dict:
    key_of = jax.random.split(jax.random.key(seed), 10)
    fields = normal_values(key_of[0], (F, NZ, NY, NX), 1.0, 6.0, ((1, 8), (2, 8), (3, 4)), jnp.float32)
    diffusivity = jnp.clip(jnp.exp(math.log(0.08) - 2.0794415 * jax.random.uniform(key_of[1], (NZ, NY, NX), jnp.float32) ** levels(key_of[1], (NZ, NY, NX), ((0, 8), (1, 8), (2, 4)), -0.2, 0.2)), 0.01, 0.08)
    courant = jnp.clip(jax.random.uniform(key_of[2], (F, 3), jnp.float32, 0.03, 0.1), 0.03, 0.1)
    tf_center = jnp.clip(jax.random.uniform(key_of[3], (TF,), jnp.float32, -1.5, 1.5), -1.5, 1.5)
    tf_sharp = jnp.clip(jnp.exp(jax.random.uniform(key_of[4], (TF,), jnp.float32, math.log(0.5), math.log(4.0))), 0.5, 4.0)
    tf_gain = jnp.clip(jnp.exp(jax.random.uniform(key_of[5], (TF,), jnp.float32, math.log(0.01), math.log(0.12))), 0.01, 0.12)
    tf_color = jnp.clip(jax.random.uniform(key_of[6], (3, TF), jnp.float32, 0.2, 1.0), 0.2, 1.0)
    tile_mask = draw_tile_mask(jax.random.fold_in(key_of[9], 71), 0)
    tile_perm = jax.vmap(lambda own: jax.random.permutation(own, TILES))(jax.random.split(key_of[8], NBY * NBX)).reshape((NBY, NBX, TILES)).astype(jnp.int32)
    return dict(fields=fields, diffusivity=diffusivity, courant=courant, tf_center=tf_center, tf_sharp=tf_sharp, tf_gain=tf_gain, tf_color=tf_color, tile_mask=tile_mask, tile_perm=tile_perm)


def inner(source, leading, axis_pos, offset):
    picks = [slice(None)] * leading + [slice(1, -1)] * 3
    length = source.shape[leading + axis_pos]
    picks[leading + axis_pos] = slice(1 + offset, length - 1 + offset)
    return source[tuple(picks)]

def advance(padded, kappa_pad, courant):
    center = inner(padded, 1, 0, 0)
    kappa_mid = inner(kappa_pad, 0, 0, 0)
    result = center
    for axis_pos in range(3):
        upper = inner(padded, 1, axis_pos, 1)
        lower = inner(padded, 1, axis_pos, -1)
        kappa_up = inner(kappa_pad, 0, axis_pos, 1)
        kappa_down = inner(kappa_pad, 0, axis_pos, -1)
        speed = courant[:, axis_pos][:, None, None, None]
        result = result + 0.5 * (kappa_mid + kappa_up) * (upper - center) + 0.5 * (kappa_mid + kappa_down) * (lower - center) - speed * (center - lower)
    return result

def reference(fields, diffusivity, courant, tf_center, tf_sharp, tf_gain, tf_color, tile_mask, tile_perm):
    kappa_pad = jnp.pad(diffusivity, 1)
    state = fields
    for level in range(2):
        state = advance(jnp.pad(state, ((0, 0), (1, 1), (1, 1), (1, 1))), kappa_pad, courant)
    scalar = state[0]
    spad = jnp.pad(scalar, 1)
    grad_z = 0.5 * (spad[2:, 1:-1, 1:-1] - spad[:-2, 1:-1, 1:-1])
    grad_y = 0.5 * (spad[1:-1, 2:, 1:-1] - spad[1:-1, :-2, 1:-1])
    grad_x = 0.5 * (spad[1:-1, 1:-1, 2:] - spad[1:-1, 1:-1, :-2])
    shade = 0.35 + 0.65 * jnp.abs(0.64 * grad_z + 0.6 * grad_y + 0.48 * grad_x) / jnp.sqrt(grad_z * grad_z + grad_y * grad_y + grad_x * grad_x + 1.0)
    modul = 1.0 + 0.5 * jnp.tanh(state[4])
    bases = [(shade * jax.nn.sigmoid(state[1 + k])).reshape(SLABS, CZ, NY, NX) for k in range(3)]
    masks = jnp.transpose(tile_mask, (1, 0, 2, 3))

    def render(items):
        center, sharp, gain, color, mask_t = items
        depth = gain * jnp.exp(-sharp * (scalar - center) ** 2) * modul
        depth = depth.reshape(SLABS, CZ, NY, NX)
        before = jnp.cumsum(depth, axis=1) - depth
        weight = jnp.exp(-before) * (1.0 - jnp.exp(-depth))
        cover = jnp.repeat(mask_t, CX, axis=2).astype(jnp.float32)
        colors = jnp.stack([lax.optimization_barrier(jnp.sum(weight * bases[k], axis=1)) * color[k] for k in range(3)], 0) * cover[None]
        alpha = (1.0 - jnp.exp(-lax.optimization_barrier(jnp.sum(depth, axis=1)))) * cover
        acc_c = colors[:, 0]
        acc_a = alpha[0]
        for slab in range(1, SLABS):
            acc_c = acc_c + (1.0 - acc_a)[None] * colors[:, slab]
            acc_a = acc_a + (1.0 - acc_a) * alpha[slab]
        return jnp.concatenate([acc_c, acc_a[None]], 0)
    image = lax.map(render, (tf_center, tf_sharp, tf_gain, tf_color.T, masks))
    tiles = image.reshape(TF, 4, NBY, CY, NBX, CX)
    tiles = jnp.transpose(tiles, (2, 4, 0, 3, 1, 5)).reshape(NBY, NBX, TF * CY, 4, CX)
    picture = jax.vmap(jax.vmap(lambda table, order: table[order]))(tiles, tile_perm)
    return (state, picture)
```

```python
import functools
import math

import jax
import jax.numpy as jnp
from jax import lax
from jax.experimental import pallas as pl
from jax.experimental.pallas import tpu as pltpu
from jax.sharding import PartitionSpec as P

MESH = pl.DeviceIdType.MESH
LOG2E = math.log2(math.e)
NF, CZ, CY, CX, TF = 5, 32, 16, 128, 16
R0 = 8
TILES = TF * CY


def kernel(
    fields, kappa, courant, center, sharp, gain, color, mask, perm,
    adv_out, pic_out,
    u0, u1, u2, sp, ysend1, yhalo1, xsend1, xhalo1, ysend2, yhalo2, xsend2, xhalo2,
    ysend3, yhalo3, xsend3, xhalo3, rs, rm, rb, tiles, recv,
    send_sem, recv_sem, tile_send, tile_recv, local_sem,
):
    f32 = jnp.float32
    nz = lax.axis_size("gz")
    sizes = [lax.axis_size(a) for a in ("gz", "gy", "gx")]
    mes = [lax.axis_index(a) for a in ("gz", "gy", "gx")]
    names = ("gz", "gy", "gx")
    per_owner = TILES // nz

    load_f = pltpu.make_async_copy(fields, u0.at[pl.ds(0, NF), pl.ds(1, CZ), pl.ds(R0, CY), :], local_sem.at[0])
    load_k = pltpu.make_async_copy(kappa, u0.at[NF, pl.ds(1, CZ), pl.ds(R0, CY), :], local_sem.at[1])
    load_f.start()
    load_k.start()

    barrier = pltpu.get_barrier_semaphore()
    count = jnp.int32(nz - 1)
    for off in range(1, nz):
        pl.semaphore_signal(
            barrier, inc=1, device_id={"gz": lax.rem(mes[0] + off, nz)}, device_id_type=MESH
        )
    for a in (1, 2):
        for step in (-1, 1):
            ok = (mes[a] > 0) if step < 0 else (mes[a] < sizes[a] - 1)

            @pl.when(ok)
            def _(a=a, step=step):
                pl.semaphore_signal(
                    barrier, inc=1, device_id={names[a]: mes[a] + step}, device_id_type=MESH
                )

            count = count + ok.astype(jnp.int32)
    pl.semaphore_wait(barrier, count)

    def exists(a, side):
        return (mes[a] > 0) if side == 0 else (mes[a] < sizes[a] - 1)

    class Face:
        def __init__(self, a, side, sem, src, dst):
            self.a, self.side, self.sem, self.src, self.dst = a, side, sem, src, dst

        def desc(self):
            a, side = self.a, self.side
            return pltpu.make_async_remote_copy(
                src_ref=self.src, dst_ref=self.dst,
                send_sem=send_sem.at[self.sem], recv_sem=recv_sem.at[self.sem],
                device_id={names[a]: mes[a] + (-1 if side == 0 else 1)}, device_id_type=MESH,
            )

        def start(self):
            @pl.when(exists(self.a, self.side))
            def _():
                self.desc().start()

        def wait_recv(self, zero):
            got = exists(self.a, 1 - self.side)

            @pl.when(got)
            def _():
                self.desc().wait_recv()

            @pl.when(jnp.logical_not(got))
            def _():
                zero()

        def wait_send(self):
            @pl.when(exists(self.a, self.side))
            def _():
                self.desc().wait_send()

    def zero_of(ref):
        def zero():
            ref[...] = jnp.zeros(ref.shape, f32)
        return zero

    lane = lax.broadcasted_iota(jnp.int32, (8, 128), 1)
    sub = lax.broadcasted_iota(jnp.int32, (8, 128), 0)
    pair = lax.bitwise_and(lax.shift_right_logical(lane + 1, 1), 63)
    even = lax.bitwise_and(lane, 1) == 0
    first_lane, last_lane = lane == 0, lane == CX - 1
    first_row, last_row = sub == 0, sub == 7

    def rolled(x, shift):
        return pltpu.roll(x, shift, 1)

    def packed(value, into, v):
        return jnp.where(pair == v, rolled(value, 2 * v), into)

    def halo_pack(ref, f):
        return jnp.where(even, rolled(ref[0, f], 1), rolled(ref[1, f], CX - 1))

    waits = []

    def faces(buf, sem, ysend, yhalo, xsend, xhalo, z_list):
        out = []
        for i, (side, src, dst) in enumerate(z_list):
            out.append((Face(0, side, sem + i, src, dst), dst))
        base = sem + len(z_list)
        for side in (0, 1):
            out.append((Face(1, side, base + side, ysend.at[side], yhalo.at[1 - side]), yhalo.at[1 - side]))
            out.append((Face(2, side, base + 2 + side, xsend.at[side], xhalo.at[1 - side]), xhalo.at[1 - side]))
        return out

    rows = pl.ds(R0, CY)
    r1 = faces(
        u0, 0, ysend1, yhalo1, xsend1, xhalo1,
        [
            (0, fields.at[:, 0], u0.at[pl.ds(0, NF), CZ + 1, rows, :]),
            (1, fields.at[:, CZ - 1], u0.at[pl.ds(0, NF), 0, rows, :]),
            (0, kappa.at[0], u0.at[NF, CZ + 1, rows, :]),
            (1, kappa.at[CZ - 1], u0.at[NF, 0, rows, :]),
        ],
    )
    for face, _ in r1[:4]:
        face.start()
    load_f.wait()
    load_k.wait()

    def pack1(z, q):
        q = list(q)
        for f in range(NF + 1):
            ysend1[0, f, pl.ds(z, 1), :] = u0[f, z + 1, pl.ds(R0, 1), :]
            ysend1[1, f, pl.ds(z, 1), :] = u0[f, z + 1, pl.ds(R0 + CY - 1, 1), :]
            for h in range(2):
                q[f] = packed(u0[f, z + 1, pl.ds(R0 + 8 * h, 8), :], q[f], 2 * z + h)
        return tuple(q)

    q = lax.fori_loop(0, CZ, pack1, tuple(jnp.zeros((8, 128), f32) for _ in range(NF + 1)))
    for f in range(NF + 1):
        xsend1[0, f] = q[f]
        xsend1[1, f] = q[f]
    for face, _ in r1[4:]:
        face.start()
    for face, dst in r1:
        face.wait_recv(zero_of(dst))
    waits += r1

    def advance(src, yhalo, xhalo, emit):
        kp = 0.5 * halo_pack(xhalo1, NF)
        fp = [halo_pack(xhalo, f) for f in range(NF)]
        cz = [courant[f, 0] for f in range(NF)]
        cy = [courant[f, 1] for f in range(NF)]
        cx = [courant[f, 2] for f in range(NF)]
        rest = [1.0 - (cz[f] + cy[f] + cx[f]) for f in range(NF)]

        def around(ref, f, z, h, yh, pack, shift, scale):
            row = R0 + 8 * h
            mid = ref[f, z + 1, pl.ds(row, 8), :]
            zm = ref[f, z, pl.ds(row, 8), :]
            zp = ref[f, z + 2, pl.ds(row, 8), :]
            ym = ref[f, z + 1, pl.ds(row - 1, 8), :]
            yp = ref[f, z + 1, pl.ds(row + 1, 8), :]
            if h == 0:
                ym = jnp.where(first_row, jnp.broadcast_to(yh[0, f, pl.ds(z, 1), :], (8, 128)), ym)
            else:
                yp = jnp.where(last_row, jnp.broadcast_to(yh[1, f, pl.ds(z, 1), :], (8, 128)), yp)
            if scale:
                mid, zm, zp, ym, yp = [0.5 * w for w in (mid, zm, zp, ym, yp)]
            edge = rolled(pack, shift)
            xm = jnp.where(first_lane, edge, rolled(mid, 1))
            xp = jnp.where(last_lane, edge, rolled(mid, CX - 1))
            return mid, zm, zp, ym, yp, xm, xp

        def body(z, q):
            q = list(q)
            for h in range(2):
                v = 2 * z + h
                shift = lax.rem(128 - 2 * v, 128)
                k = around(u0, NF, z, h, yhalo1, kp, shift, True)
                kzm, kzp, kym, kyp, kxm, kxp = [k[0] + w for w in k[1:]]
                ksum = (kzm + kzp) + (kym + kyp) + (kxm + kxp)
                for f in range(NF):
                    mid, zm, zp, ym, yp, xm, xp = around(src, f, z, h, yhalo, fp[f], shift, False)
                    value = (
                        (rest[f] - ksum) * mid
                        + (kzp * zp + (kzm + cz[f]) * zm)
                        + (kyp * yp + (kym + cy[f]) * ym)
                        + (kxp * xp + (kxm + cx[f]) * xm)
                    )
                    emit(f, z, h, value)
                    q[f] = packed(value, q[f], v)
            return tuple(q)

        return lax.fori_loop(0, CZ, body, tuple(jnp.zeros((8, 128), f32) for _ in range(NF)))

    def emit1(f, z, h, value):
        u1[f, z + 1, pl.ds(R0 + 8 * h, 8), :] = value
        side, row = (0, 0) if h == 0 else (1, 7)
        ysend2[side, f, pl.ds(z, 1), :] = value[row : row + 1, :]

    q = advance(u0, yhalo1, xhalo1, emit1)
    for f in range(NF):
        xsend2[0, f] = q[f]
        xsend2[1, f] = q[f]
    r2 = faces(
        u1, 8, ysend2, yhalo2, xsend2, xhalo2,
        [
            (0, u1.at[:, 1, rows, :], u1.at[:, CZ + 1, rows, :]),
            (1, u1.at[:, CZ, rows, :], u1.at[:, 0, rows, :]),
        ],
    )
    for face, _ in r2:
        face.start()
    for face, dst in r2:
        face.wait_recv(zero_of(dst))
    waits += r2

    def emit2(f, z, h, value):
        u2[f, z, pl.ds(8 * h, 8), :] = value
        if f == 0:
            sp[z + 1, pl.ds(R0 + 8 * h, 8), :] = value
            side, row = (0, 0) if h == 0 else (1, 7)
            ysend3[side, 0, pl.ds(z, 1), :] = value[row : row + 1, :]

    q = advance(u1, yhalo2, xhalo2, emit2)
    xsend3[0, 0] = q[0]
    xsend3[1, 0] = q[0]
    r3 = faces(
        sp, 14, ysend3, yhalo3, xsend3, xhalo3,
        [
            (0, sp.at[1, rows, :], sp.at[CZ + 1, rows, :]),
            (1, sp.at[CZ, rows, :], sp.at[0, rows, :]),
        ],
    )
    for face, _ in r3:
        face.start()
    store = pltpu.make_async_copy(u2, adv_out, local_sem.at[2])
    store.start()

    def sites(z, h):
        start = h * 8 * CZ + lax.rem(z, 4) * 8 + lax.div(z, 4)
        return pl.ds(start, 8, stride=CZ)

    rs2, rm2 = rs.reshape(CY * CZ, CX), rm.reshape(CY * CZ, CX)
    rb2 = rb.reshape(3, CY * CZ, CX)

    def modulate(z, carry):
        for h in range(2):
            at = sites(z, h)
            rs2[at, :] = u2[0, z, pl.ds(8 * h, 8), :]
            rm2[at, :] = (-LOG2E) * (1.0 + 0.5 * jnp.tanh(u2[4, z, pl.ds(8 * h, 8), :]))
        return carry

    lax.fori_loop(0, CZ, modulate, 0)
    for face, dst in r3:
        face.wait_recv(zero_of(dst))
    waits += r3

    spack = halo_pack(xhalo3, 0)

    def shading(z, carry):
        for h in range(2):
            row = R0 + 8 * h
            v = 2 * z + h
            mid = sp[z + 1, pl.ds(row, 8), :]
            ym = sp[z + 1, pl.ds(row - 1, 8), :]
            yp = sp[z + 1, pl.ds(row + 1, 8), :]
            if h == 0:
                ym = jnp.where(first_row, jnp.broadcast_to(yhalo3[0, 0, pl.ds(z, 1), :], (8, 128)), ym)
            else:
                yp = jnp.where(last_row, jnp.broadcast_to(yhalo3[1, 0, pl.ds(z, 1), :], (8, 128)), yp)
            edge = rolled(spack, lax.rem(128 - 2 * v, 128))
            xm = jnp.where(first_lane, edge, rolled(mid, 1))
            xp = jnp.where(last_lane, edge, rolled(mid, CX - 1))
            gz = 0.5 * (sp[z + 2, pl.ds(row, 8), :] - sp[z, pl.ds(row, 8), :])
            gy = 0.5 * (yp - ym)
            gx = 0.5 * (xp - xm)
            shade = 0.35 + 0.65 * jnp.abs(0.64 * gz + 0.6 * gy + 0.48 * gx) * lax.rsqrt(
                gz * gz + gy * gy + gx * gx + 1.0
            )
            at = sites(z, h)
            for k in range(3):
                rb2[k, at, :] = shade * jax.nn.sigmoid(u2[1 + k, z, pl.ds(8 * h, 8), :])
        return carry

    lax.fori_loop(0, CZ, shading, 0)

    def owner_copy(k, owner):
        return pltpu.make_async_remote_copy(
            src_ref=tiles.at[k], dst_ref=recv.at[mes[0]],
            send_sem=tile_send.at[k], recv_sem=tile_recv.at[mes[0]],
            device_id={"gz": owner}, device_id_type=MESH,
        )

    def render(owner, dst):
        def one(i, carry):
            p = perm[0, 0, owner * per_owner + i]
            t = lax.shift_right_logical(p, 4)
            y = lax.bitwise_and(p, 15)
            cover = mask[0, t, y, 0].astype(f32)
            mid, slope, amount = center[t], -LOG2E * sharp[t], gain[t]
            gap = rs[y] - mid
            depth = jnp.exp2(slope * (gap * gap)) * (amount * rm[y])
            e = [depth[0:8]]
            for w in range(1, 4):
                e.append(e[-1] + depth[8 * w : 8 * w + 8])
            inclusive = e[3]
            for sh in (1, 2, 4):
                inclusive = inclusive + jnp.where(sub >= sh, pltpu.roll(inclusive, sh, 0), 0.0)
            before = jnp.exp2(inclusive - e[3])
            lit = [jnp.exp2(x) for x in e]
            weight = [1.0 - lit[0]] + [lit[w] - lit[w + 1] for w in range(3)]
            for k in range(3):
                base = rb[k, y]
                total = weight[0] * base[0:8]
                for w in range(1, 4):
                    total = total + weight[w] * base[8 * w : 8 * w + 8]
                total = jnp.sum(total * before, axis=0, keepdims=True)
                dst[k, pl.ds(i, 1), :] = total * (color[k, t] * cover)
            dst[3, pl.ds(i, 1), :] = (1.0 - jnp.exp2(inclusive[7:8])) * cover
            return carry

        lax.fori_loop(0, per_owner, one, 0, unroll=2)

    offs = sorted(range(1, nz), key=lambda o: -min(o, nz - o))
    for k, off in enumerate(offs):
        owner = lax.rem(mes[0] + off, nz)
        render(owner, tiles.at[k])
        owner_copy(k, owner).start()
    render(mes[0], recv.at[mes[0]])

    for off in offs:
        src = lax.rem(mes[0] + nz - off, nz)
        pltpu.make_async_remote_copy(
            src_ref=tiles.at[0], dst_ref=recv.at[src], send_sem=tile_send.at[0], recv_sem=tile_recv.at[src],
            device_id={"gz": src}, device_id_type=MESH,
        ).wait_recv()

    def composite(i, carry):
        at = pl.ds(pl.multiple_of(8 * i, 8), 8)
        acc = [recv[0, k, at, :] for k in range(4)]
        for s in range(1, nz):
            clear = 1.0 - acc[3]
            acc = [acc[k] + clear * recv[s, k, at, :] for k in range(4)]
        for k in range(4):
            for r in range(8):
                pic_out[0, 0, 8 * i + r, pl.ds(k, 1), :] = acc[k][r : r + 1, :]
        return carry

    lax.fori_loop(0, per_owner // 8, composite, 0)
    for k, off in enumerate(offs):
        owner_copy(k, lax.rem(mes[0] + off, nz)).wait_send()
    for face, _ in waits:
        face.wait_send()
    store.wait()


def shards(fields, diffusivity, courant, tf_center, tf_sharp, tf_gain, tf_color, tile_mask, tile_perm):
    nz = lax.axis_size("gz")
    per_owner = TILES // nz
    f32 = jnp.float32
    smem = pl.BlockSpec(memory_space=pltpu.SMEM)
    vm = pltpu.VMEM
    halo = lambda n: [vm((2, n, CZ, CX), f32), vm((2, n, CZ, CX), f32), vm((2, n, 8, CX), f32), vm((2, n, 8, CX), f32)]
    return pl.pallas_call(
        kernel,
        out_shape=(
            jax.ShapeDtypeStruct((NF, CZ, CY, CX), f32),
            jax.ShapeDtypeStruct((1, 1, per_owner, 4, CX), f32),
        ),
        in_specs=[pl.BlockSpec(memory_space=pl.ANY)] * 2 + [smem] * 7,
        out_specs=(pl.BlockSpec(memory_space=pl.ANY), pl.BlockSpec(memory_space=pltpu.VMEM)),
        scratch_shapes=[
            vm((NF + 1, CZ + 2, 32, CX), f32),
            vm((NF, CZ + 2, 32, CX), f32),
            vm((NF, CZ, CY, CX), f32),
            vm((CZ + 2, 32, CX), f32),
            *halo(NF + 1), *halo(NF), *halo(1),
            vm((CY, CZ, CX), f32),
            vm((CY, CZ, CX), f32),
            vm((3, CY, CZ, CX), f32),
            vm((max(nz - 1, 1), 4, per_owner, CX), f32),
            vm((nz, 4, per_owner, CX), f32),
            pltpu.SemaphoreType.DMA((20,)),
            pltpu.SemaphoreType.DMA((20,)),
            pltpu.SemaphoreType.DMA((nz,)),
            pltpu.SemaphoreType.DMA((nz,)),
            pltpu.SemaphoreType.DMA((3,)),
        ],
        compiler_params=pltpu.CompilerParams(collective_id=0, has_side_effects=True),
        name="insitu",
    )(fields, diffusivity, courant, tf_center, tf_sharp, tf_gain, tf_color, tile_mask, tile_perm)


def solution(mesh):
    return jax.shard_map(
        shards,
        mesh=mesh,
        in_specs=(
            P(None, "gz", "gy", "gx"),
            P("gz", "gy", "gx"),
            P(),
            P(),
            P(),
            P(),
            P(),
            P("gz", None, "gy", "gx"),
            P("gy", "gx", None),
        ),
        out_specs=(P(None, "gz", "gy", "gx"), P("gy", "gx", "gz", None, None)),
        check_vma=False,
    )
```

```python
import functools
import math

import jax
import jax.numpy as jnp
from jax import lax
from jax.experimental import pallas as pl
from jax.experimental.pallas import tpu as pltpu
from jax.sharding import PartitionSpec as P

MESH = pl.DeviceIdType.MESH
LOG2E = math.log2(math.e)
NF, CZ, CY, CX, TF = 5, 32, 16, 128, 16
R0 = 8
TILES = TF * CY
GROUPS1 = ((0, 2), (2, 3))
GROUPS2 = ((0, 1), (1, 2), (3, 2))
UNROLL = 8


def kernel(
    fields, kappa, courant_in, center_in, sharp_in, gain_in, color_in, mask_in, perm_in,
    u2, pic_out,
    kb, u0, u1, sp, ysendk, yhalok, xsendk, xhalok, ysend1, yhalo1, xsend1, xhalo1,
    ysend2, yhalo2, xsend2, xhalo2, ysend3, yhalo3, xsend3, xhalo3,
    kz, kf, sig, rs, rm, rb, tiles, recv,
    courant, center, sharp, gain, color, mask, perm,
    send_sem, recv_sem, tile_send, tile_recv, local_sem, token,
):
    f32 = jnp.float32
    names = ("gz", "gy", "gx")
    sizes = [lax.axis_size(a) for a in names]
    mes = [lax.axis_index(a) for a in names]
    nz = sizes[0]
    per_owner = TILES // nz
    rows = pl.ds(R0, CY)

    def local(i, src, dst):
        copy = pltpu.make_async_copy(src, dst, local_sem.at[i])
        copy.start()
        return copy

    load_k = local(0, kappa, kb.at[pl.ds(1, CZ), rows, :])
    loads = [local(1 + f, fields.at[f], u0.at[f, pl.ds(1, CZ), rows, :]) for f in range(NF)]
    small = [
        local(6 + i, a, b)
        for i, (a, b) in enumerate(
            zip(
                (courant_in, center_in, sharp_in, gain_in, color_in, mask_in, perm_in),
                (courant, center, sharp, gain, color, mask, perm),
            )
        )
    ]

    def exists(a, side):
        return (mes[a] > 0) if side == 0 else (mes[a] < sizes[a] - 1)

    ring = [lax.rem(mes[0] + 1, nz), lax.rem(mes[0] + nz - 1, nz)]
    barrier = pltpu.get_barrier_semaphore()

    def greet(sem):
        for z in ring:
            pl.semaphore_signal(sem, inc=1, device_id={"gz": z}, device_id_type=MESH)

    greet(barrier)
    count = jnp.int32(2)
    for a in (1, 2):
        for side in (0, 1):
            ok = exists(a, side)

            @pl.when(ok)
            def _(a=a, side=side):
                pl.semaphore_signal(
                    barrier, inc=1, device_id={names[a]: mes[a] + 2 * side - 1}, device_id_type=MESH
                )

            count = count + ok.astype(jnp.int32)

    lane = lax.broadcasted_iota(jnp.int32, (8, 128), 1)
    sub = lax.broadcasted_iota(jnp.int32, (8, 128), 0)
    pair = lax.bitwise_and(lax.shift_right_logical(lane + 1, 1), 63)
    even = lax.bitwise_and(lane, 1) == 0
    first_lane, last_lane = lane == 0, lane == CX - 1
    first_row, last_row = sub == 0, sub == 7
    blank = jnp.zeros((8, 128), f32)

    def rolled(x, shift):
        return pltpu.roll(x, shift, 1)

    def packed(value, into, v):
        return jnp.where(pair == v, rolled(value, 2 * v), into)

    def halo_pack(ref, f):
        return jnp.where(even, rolled(ref[0, f], 1), rolled(ref[1, f], CX - 1))

    for a, side, refs in (
        (0, 0, (kb.at[0, rows, :], u0.at[:, 0, rows, :], u1.at[:, 0, rows, :], sp.at[0, rows, :])),
        (0, 1, (kb.at[CZ + 1, rows, :], u0.at[:, CZ + 1, rows, :], u1.at[:, CZ + 1, rows, :], sp.at[CZ + 1, rows, :])),
        *((1, s, tuple(r.at[s] for r in (yhalok, yhalo1, yhalo2, yhalo3))) for s in (0, 1)),
        *((2, s, tuple(r.at[s] for r in (xhalok, xhalo1, xhalo2, xhalo3))) for s in (0, 1)),
    ):

        @pl.when(jnp.logical_not(exists(a, side)))
        def _(refs=refs):
            for r in refs:
                r[...] = jnp.zeros(r.shape, f32)

    class Faces:
        def __init__(self, sem, parts):
            self.sem, self.parts = sem, parts

        def desc(self, a, side):
            src, dst = self.parts[2 * a + side]
            i = self.sem + 2 * a + side
            return pltpu.make_async_remote_copy(
                src_ref=src, dst_ref=dst, send_sem=send_sem.at[i], recv_sem=recv_sem.at[i],
                device_id={names[a]: mes[a] + 2 * side - 1}, device_id_type=MESH,
            )

        def each(self, what, incoming):
            for a in (1, 2, 0):
                for side in (0, 1):

                    @pl.when(exists(a, 1 - side if incoming else side))
                    def _(a=a, side=side):
                        getattr(self.desc(a, side), what)()

        def start(self):
            self.each("start", False)

        def wait_recv(self):
            self.each("wait_recv", True)

        def wait_send(self):
            self.each("wait_send", False)

    def yx_parts(ys, yh, xs, xh, at):
        return [
            (ys.at[0, at], yh.at[1, at]), (ys.at[1, at], yh.at[0, at]),
            (xs.at[at], xh.at[1, at]), (xs.at[at], xh.at[0, at]),
        ]

    one = pl.ds(0, 1)
    facesk = Faces(0, [
        (kappa.at[0], kb.at[CZ + 1, rows, :]), (kappa.at[CZ - 1], kb.at[0, rows, :]),
        *yx_parts(ysendk, yhalok, xsendk, xhalok, one),
    ])
    faces1, faces2 = [], []
    for g, (f, n) in enumerate(GROUPS1):
        at = pl.ds(f, n)
        faces1.append(Faces(6 + 6 * g, [
            (fields.at[at, 0], u0.at[at, CZ + 1, rows, :]), (fields.at[at, CZ - 1], u0.at[at, 0, rows, :]),
            *yx_parts(ysend1, yhalo1, xsend1, xhalo1, at),
        ]))
    for g, (f, n) in enumerate(GROUPS2):
        at = pl.ds(f, n)
        faces2.append(Faces(18 + 6 * g, [
            (u1.at[at, 1, rows, :], u1.at[at, CZ + 1, rows, :]), (u1.at[at, CZ, rows, :], u1.at[at, 0, rows, :]),
            *yx_parts(ysend2, yhalo2, xsend2, xhalo2, at),
        ]))
    faces3 = Faces(36, [
        (sp.at[1, rows, :], sp.at[CZ + 1, rows, :]), (sp.at[CZ, rows, :], sp.at[0, rows, :]),
        *yx_parts(ysend3, yhalo3, xsend3, xhalo3, one),
    ])

    def sweep(body, init):
        def step(i, carry):
            for j in range(UNROLL):
                carry = body(UNROLL * i + j, carry)
            return carry

        return lax.fori_loop(0, CZ // UNROLL, step, init)

    def pack_planes(ref, ysend, xsend, f):
        def body(z, q):
            ysend[0, f, pl.ds(z, 1), :] = ref[z + 1, pl.ds(R0, 1), :]
            ysend[1, f, pl.ds(z, 1), :] = ref[z + 1, pl.ds(R0 + CY - 1, 1), :]
            for h in range(2):
                q = packed(ref[z + 1, pl.ds(R0 + 8 * h, 8), :], q, 2 * z + h)
            return q

        xsend[f] = sweep(body, blank)

    load_k.wait()
    pack_planes(kb, ysendk, xsendk, 0)
    for f in range(NF):
        loads[f].wait()
        pack_planes(u0.at[f], ysend1, xsend1, f)
    for copy in small:
        copy.wait()
    pl.semaphore_wait(barrier, count)
    facesk.start()
    for face in faces1:
        face.start()
    greet(token.at[0])

    def sides(ref, z, h, yhalo, f, pack):
        row = R0 + 8 * h
        mid = ref[z + 1, pl.ds(row, 8), :]
        zm, zp = ref[z, pl.ds(row, 8), :], ref[z + 2, pl.ds(row, 8), :]
        ym, yp = ref[z + 1, pl.ds(row - 1, 8), :], ref[z + 1, pl.ds(row + 1, 8), :]
        if h == 0:
            ym = jnp.where(first_row, jnp.broadcast_to(yhalo[0, f, pl.ds(z, 1), :], (8, 128)), ym)
        else:
            yp = jnp.where(last_row, jnp.broadcast_to(yhalo[1, f, pl.ds(z, 1), :], (8, 128)), yp)
        edge = rolled(pack, lax.rem(128 - 2 * (2 * z + h), 128))
        xm = jnp.where(first_lane, edge, rolled(mid, 1))
        xp = jnp.where(last_lane, edge, rolled(mid, CX - 1))
        return mid, zm, zp, ym, yp, xm, xp

    facesk.wait_recv()
    kpack = halo_pack(xhalok, 0)

    def coefficients(z, carry):
        for h in range(2):
            at = pl.ds(8 * h, 8)
            mid, *others = sides(kb, z, h, yhalok, 0, kpack)
            means = [0.5 * (mid + w) for w in others]
            kz[z, at, :] = means[0]
            kz[z + 1, at, :] = means[1]
            for i in range(4):
                kf[i, z, at, :] = means[2 + i]
            kf[4, z, at, :] = 1.0 - ((means[0] + means[1]) + (means[2] + means[3]) + (means[4] + means[5]))
        return carry

    sweep(coefficients, 0)

    def advance(src, f, yhalo, xhalo, emit):
        pack = halo_pack(xhalo, f)
        cz, cy, cx = courant[0, f], courant[1, f], courant[2, f]
        total = cz + cy + cx

        def body(z, q):
            for h in range(2):
                at = pl.ds(8 * h, 8)
                mid, zm, zp, ym, yp, xm, xp = sides(src.at[f], z, h, yhalo, f, pack)
                value = (
                    (kf[4, z, at, :] - total) * mid
                    + (kz[z + 1, at, :] * zp + (kz[z, at, :] + cz) * zm)
                    + (kf[1, z, at, :] * yp + (kf[0, z, at, :] + cy) * ym)
                    + (kf[3, z, at, :] * xp + (kf[2, z, at, :] + cx) * xm)
                )
                emit(z, h, value)
                if q is not None:
                    q = packed(value, q, 2 * z + h)
            return q

        return body

    def step1(f):
        def emit(z, h, value):
            u1[f, z + 1, pl.ds(R0 + 8 * h, 8), :] = value
            side, row = (0, 0) if h == 0 else (1, 7)
            ysend2[side, f, pl.ds(z, 1), :] = value[row : row + 1, :]

        xsend2[f] = sweep(advance(u0, f, yhalo1, xhalo1, emit), blank)

    arrivals1 = {f: faces1[g] for g, (f, n) in enumerate(GROUPS1)}
    departures2 = {f + n - 1: faces2[g] for g, (f, n) in enumerate(GROUPS2)}
    for f in range(NF):
        if f in arrivals1:
            arrivals1[f].wait_recv()
        step1(f)
        if f in departures2:
            departures2[f].start()
    pl.semaphore_wait(token.at[0], 2)
    greet(token.at[1])

    def sites(z, h):
        start = h * 8 * CZ + lax.rem(z, 4) * 8 + lax.div(z, 4)
        return pl.ds(start, 8, stride=CZ)

    rs2, rm2 = rs.reshape(CY * CZ, CX), rm.reshape(CY * CZ, CX)
    rb2 = rb.reshape(3, CY * CZ, CX)

    def step2(f):
        def emit(z, h, value):
            at = pl.ds(8 * h, 8)
            u2[f, z, at, :] = value
            if f == 0:
                sp[z + 1, pl.ds(R0 + 8 * h, 8), :] = value
                side, row = (0, 0) if h == 0 else (1, 7)
                ysend3[side, 0, pl.ds(z, 1), :] = value[row : row + 1, :]
                rs2[sites(z, h), :] = value
            elif f == 4:
                rm2[sites(z, h), :] = (-LOG2E) - (0.5 * LOG2E) * jnp.tanh(value)
            else:
                sig[f - 1, z, at, :] = 0.5 + 0.5 * jnp.tanh(0.5 * value)

        out = sweep(advance(u1, f, yhalo2, xhalo2, emit), blank if f == 0 else None)
        if f == 0:
            xsend3[0] = out

    arrivals2 = {f: faces2[g] for g, (f, n) in enumerate(GROUPS2)}
    for f in range(NF):
        if f in arrivals2:
            arrivals2[f].wait_recv()
        step2(f)
        if f == 0:
            faces3.start()
            pl.semaphore_wait(token.at[1], 2)
            greet(token.at[2])

    faces3.wait_recv()
    spack = halo_pack(xhalo3, 0)

    def shading(z, carry):
        for h in range(2):
            _, zm, zp, ym, yp, xm, xp = sides(sp, z, h, yhalo3, 0, spack)
            gz, gy, gx = 0.5 * (zp - zm), 0.5 * (yp - ym), 0.5 * (xp - xm)
            shade = 0.35 + 0.65 * jnp.abs(0.64 * gz + 0.6 * gy + 0.48 * gx) * lax.rsqrt(
                gz * gz + gy * gy + gx * gx + 1.0
            )
            for k in range(3):
                rb2[k, sites(z, h), :] = shade * sig[k, z, pl.ds(8 * h, 8), :]
        return carry

    sweep(shading, 0)
    pl.semaphore_wait(token.at[2], 2)

    def owner_copy(k, owner):
        return pltpu.make_async_remote_copy(
            src_ref=tiles.at[k], dst_ref=recv.at[mes[0]],
            send_sem=tile_send.at[k], recv_sem=tile_recv.at[mes[0]],
            device_id={"gz": owner}, device_id_type=MESH,
        )

    def render(owner, dst):
        def tile(i, carry):
            p = perm[0, 0, owner * per_owner + i]
            t = lax.shift_right_logical(p, 4)
            y = lax.bitwise_and(p, 15)
            cover = mask[0, t, 0, y].astype(f32)
            mid, slope, amount = center[t], -LOG2E * sharp[t], gain[t]
            gap = rs[y] - mid
            depth = jnp.exp2(slope * (gap * gap)) * (amount * rm[y])
            e = [depth[0:8]]
            for w in range(1, 4):
                e.append(e[-1] + depth[8 * w : 8 * w + 8])
            inclusive = e[3]
            for sh in (1, 2, 4):
                inclusive = inclusive + jnp.where(sub >= sh, pltpu.roll(inclusive, sh, 0), 0.0)
            before = jnp.exp2(inclusive - e[3])
            lit = [jnp.exp2(x) for x in e]
            weight = [1.0 - lit[0]] + [lit[w] - lit[w + 1] for w in range(3)]
            for k in range(3):
                base = rb[k, y]
                total = weight[0] * base[0:8]
                for w in range(1, 4):
                    total = total + weight[w] * base[8 * w : 8 * w + 8]
                total = jnp.sum(total * before, axis=0, keepdims=True)
                dst[k, pl.ds(i, 1), :] = total * (color[k, t] * cover)
            dst[3, pl.ds(i, 1), :] = (1.0 - jnp.exp2(inclusive[7:8])) * cover
            return carry

        lax.fori_loop(0, per_owner, tile, 0, unroll=4)

    offs = sorted(range(1, nz), key=lambda o: -min(o, nz - o))
    for k, off in enumerate(offs):
        owner = lax.rem(mes[0] + off, nz)
        render(owner, tiles.at[k])
        owner_copy(k, owner).start()
    render(mes[0], recv.at[mes[0]])

    for off in offs:
        src = lax.rem(mes[0] + nz - off, nz)
        pltpu.make_async_remote_copy(
            src_ref=tiles.at[0], dst_ref=recv.at[src], send_sem=tile_send.at[0], recv_sem=tile_recv.at[src],
            device_id={"gz": src}, device_id_type=MESH,
        ).wait_recv()

    def composite(i, carry):
        at = pl.ds(pl.multiple_of(8 * i, 8), 8)
        acc = [recv[0, k, at, :] for k in range(4)]
        for s in range(1, nz):
            clear = 1.0 - acc[3]
            acc = [acc[k] + clear * recv[s, k, at, :] for k in range(4)]
        for k in range(4):
            for r in range(8):
                pic_out[0, 0, 8 * i + r, pl.ds(k, 1), :] = acc[k][r : r + 1, :]
        return carry

    lax.fori_loop(0, per_owner // 8, composite, 0)
    for k, off in enumerate(offs):
        owner_copy(k, lax.rem(mes[0] + off, nz)).wait_send()
    for face in [facesk, *faces1, *faces2, faces3]:
        face.wait_send()


def shards(fields, diffusivity, courant, tf_center, tf_sharp, tf_gain, tf_color, tile_mask, tile_perm):
    nz = lax.axis_size("gz")
    per_owner = TILES // nz
    f32 = jnp.float32
    vm = pltpu.VMEM
    anywhere = pl.BlockSpec(memory_space=pl.ANY)
    inside = pl.BlockSpec(memory_space=pltpu.VMEM)

    def halo(n):
        return [vm((2, n, CZ, CX), f32), vm((2, n, CZ, CX), f32), vm((n, 8, CX), f32), vm((2, n, 8, CX), f32)]

    sm = lambda a: pltpu.SMEM(a.shape, a.dtype)
    operands = (
        fields, diffusivity, courant.T, tf_center, tf_sharp, tf_gain, tf_color,
        jnp.transpose(tile_mask, (0, 1, 3, 2)), tile_perm,
    )
    return pl.pallas_call(
        kernel,
        out_shape=(vm((NF, CZ, CY, CX), f32), vm((1, 1, per_owner, 4, CX), f32)),
        in_specs=[anywhere] * 9,
        out_specs=(inside, inside),
        scratch_shapes=[
            vm((CZ + 2, 32, CX), f32),
            vm((NF, CZ + 2, 32, CX), f32),
            vm((NF, CZ + 2, 32, CX), f32),
            vm((CZ + 2, 32, CX), f32),
            *halo(1), *halo(NF), *halo(NF), *halo(1),
            vm((CZ + 1, CY, CX), f32),
            vm((5, CZ, CY, CX), f32),
            vm((3, CZ, CY, CX), f32),
            vm((CY, CZ, CX), f32),
            vm((CY, CZ, CX), f32),
            vm((3, CY, CZ, CX), f32),
            vm((max(nz - 1, 1), 4, per_owner, CX), f32),
            vm((nz, 4, per_owner, CX), f32),
            *[sm(a) for a in operands[2:]],
            pltpu.SemaphoreType.DMA((42,)),
            pltpu.SemaphoreType.DMA((42,)),
            pltpu.SemaphoreType.DMA((nz,)),
            pltpu.SemaphoreType.DMA((nz,)),
            pltpu.SemaphoreType.DMA((13,)),
            pltpu.SemaphoreType.REGULAR((3,)),
        ],
        compiler_params=pltpu.CompilerParams(collective_id=0, has_side_effects=True),
        name="insitu",
    )(*operands)


def solution(mesh):
    return jax.shard_map(
        shards,
        mesh=mesh,
        in_specs=(
            P(None, "gz", "gy", "gx"),
            P("gz", "gy", "gx"),
            P(),
            P(),
            P(),
            P(),
            P(),
            P("gz", None, "gy", "gx"),
            P("gy", "gx", None),
        ),
        out_specs=(P(None, "gz", "gy", "gx"), P("gy", "gx", "gz", None, None)),
        check_vma=False,
    )
```

```python
import functools
import math

import jax
import jax.numpy as jnp
from jax import lax
from jax.experimental import pallas as pl
from jax.experimental.pallas import tpu as pltpu
from jax.sharding import PartitionSpec as P

MESH = pl.DeviceIdType.MESH
LOG2E = math.log2(math.e)
NF, CZ, CY, CX, TF = 5, 32, 16, 128, 16
R0 = 8
TILES = TF * CY
GROUPS1 = ((0, 2), (2, 3))
GROUPS2 = ((0, 1), (1, 2), (3, 2))
UNROLL = 16


def kernel(
    fields, kappa, courant_in, center_in, sharp_in, gain_in, color_in, mask_in, perm_in,
    u2, pic_out,
    kb, u0, u1, sp, ysendk, yhalok, xsendk, xhalok, ysend1, yhalo1, xsend1, xhalo1,
    ysend2, yhalo2, xsend2, xhalo2, ysend3, yhalo3, xsend3, xhalo3,
    kz, kf, rs, rm, rh, rb, mtiles, mrecv, rtiles, ptiles, precv, recv,
    courant, center, sharp, gain, color, mask, perm,
    send_sem, recv_sem, tile_send, tile_recv, local_sem, token,
):
    f32 = jnp.float32
    names = ("gz", "gy", "gx")
    sizes = [lax.axis_size(a) for a in names]
    mes = [lax.axis_index(a) for a in names]
    nz = sizes[0]
    per_owner = TILES // nz
    rows = pl.ds(R0, CY)

    def local(i, src, dst):
        copy = pltpu.make_async_copy(src, dst, local_sem.at[i])
        copy.start()
        return copy

    load_k = local(0, kappa, kb.at[pl.ds(1, CZ), rows, :])
    loads = [local(1 + f, fields.at[f], u0.at[f, pl.ds(1, CZ), rows, :]) for f in range(NF)]
    small = [
        local(6 + i, a, b)
        for i, (a, b) in enumerate(
            zip(
                (courant_in, center_in, sharp_in, gain_in, color_in, mask_in, perm_in),
                (courant, center, sharp, gain, color, mask, perm),
            )
        )
    ]

    def exists(a, side):
        return (mes[a] > 0) if side == 0 else (mes[a] < sizes[a] - 1)

    ring = [lax.rem(mes[0] + 1, nz), lax.rem(mes[0] + nz - 1, nz)]
    barrier = pltpu.get_barrier_semaphore()

    def greet(sem):
        for z in ring:
            pl.semaphore_signal(sem, inc=1, device_id={"gz": z}, device_id_type=MESH)

    greet(barrier)
    count = jnp.int32(2)
    for a in (1, 2):
        for side in (0, 1):
            ok = exists(a, side)

            @pl.when(ok)
            def _(a=a, side=side):
                pl.semaphore_signal(
                    barrier, inc=1, device_id={names[a]: mes[a] + 2 * side - 1}, device_id_type=MESH
                )

            count = count + ok.astype(jnp.int32)

    lane = lax.broadcasted_iota(jnp.int32, (8, 128), 1)
    sub = lax.broadcasted_iota(jnp.int32, (8, 128), 0)
    pair = lax.bitwise_and(lax.shift_right_logical(lane + 1, 1), 63)
    even = lax.bitwise_and(lane, 1) == 0
    first_lane, last_lane = lane == 0, lane == CX - 1
    first_row, last_row = sub == 0, sub == 7
    blank = jnp.zeros((8, 128), f32)

    def rolled(x, shift):
        return pltpu.roll(x, shift, 1)

    def packed(value, into, v):
        return jnp.where(pair == v, rolled(value, 2 * v), into)

    def halo_pack(ref, f):
        return jnp.where(even, rolled(ref[0, f], 1), rolled(ref[1, f], CX - 1))

    for a, side, refs in (
        (0, 0, (kb.at[0, rows, :], u0.at[:, 0, rows, :], u1.at[:, 0, rows, :], sp.at[0, rows, :])),
        (0, 1, (kb.at[CZ + 1, rows, :], u0.at[:, CZ + 1, rows, :], u1.at[:, CZ + 1, rows, :], sp.at[CZ + 1, rows, :])),
        *((1, s, tuple(r.at[s] for r in (yhalok, yhalo1, yhalo2, yhalo3))) for s in (0, 1)),
        *((2, s, tuple(r.at[s] for r in (xhalok, xhalo1, xhalo2, xhalo3))) for s in (0, 1)),
    ):

        @pl.when(jnp.logical_not(exists(a, side)))
        def _(refs=refs):
            for r in refs:
                r[...] = jnp.zeros(r.shape, f32)

    class Faces:
        def __init__(self, sem, parts):
            self.sem, self.parts = sem, parts

        def desc(self, a, side):
            src, dst = self.parts[2 * a + side]
            i = self.sem + 2 * a + side
            return pltpu.make_async_remote_copy(
                src_ref=src, dst_ref=dst, send_sem=send_sem.at[i], recv_sem=recv_sem.at[i],
                device_id={names[a]: mes[a] + 2 * side - 1}, device_id_type=MESH,
            )

        def each(self, what, incoming):
            for a in (1, 2, 0):
                for side in (0, 1):

                    @pl.when(exists(a, 1 - side if incoming else side))
                    def _(a=a, side=side):
                        getattr(self.desc(a, side), what)()

        def start(self):
            self.each("start", False)

        def wait_recv(self):
            self.each("wait_recv", True)

        def wait_send(self):
            self.each("wait_send", False)

    def yx_parts(ys, yh, xs, xh, at):
        return [
            (ys.at[0, at], yh.at[1, at]), (ys.at[1, at], yh.at[0, at]),
            (xs.at[at], xh.at[1, at]), (xs.at[at], xh.at[0, at]),
        ]

    one = pl.ds(0, 1)
    facesk = Faces(0, [
        (kappa.at[0], kb.at[CZ + 1, rows, :]), (kappa.at[CZ - 1], kb.at[0, rows, :]),
        *yx_parts(ysendk, yhalok, xsendk, xhalok, one),
    ])
    faces1, faces2 = [], []
    for g, (f, n) in enumerate(GROUPS1):
        at = pl.ds(f, n)
        faces1.append(Faces(6 + 6 * g, [
            (fields.at[at, 0], u0.at[at, CZ + 1, rows, :]), (fields.at[at, CZ - 1], u0.at[at, 0, rows, :]),
            *yx_parts(ysend1, yhalo1, xsend1, xhalo1, at),
        ]))
    for g, (f, n) in enumerate(GROUPS2):
        at = pl.ds(f, n)
        faces2.append(Faces(18 + 6 * g, [
            (u1.at[at, 1, rows, :], u1.at[at, CZ + 1, rows, :]), (u1.at[at, CZ, rows, :], u1.at[at, 0, rows, :]),
            *yx_parts(ysend2, yhalo2, xsend2, xhalo2, at),
        ]))
    faces3 = Faces(36, [
        (sp.at[1, rows, :], sp.at[CZ + 1, rows, :]), (sp.at[CZ, rows, :], sp.at[0, rows, :]),
        *yx_parts(ysend3, yhalo3, xsend3, xhalo3, one),
    ])

    def sweep(body, init):
        def step(i, carry):
            for j in range(UNROLL):
                carry = body(UNROLL * i + j, carry)
            return carry

        return lax.fori_loop(0, CZ // UNROLL, step, init)

    def pack_planes(ref, ysend, xsend, f):
        def body(z, q):
            ysend[0, f, pl.ds(z, 1), :] = ref[z + 1, pl.ds(R0, 1), :]
            ysend[1, f, pl.ds(z, 1), :] = ref[z + 1, pl.ds(R0 + CY - 1, 1), :]
            for h in range(2):
                q = packed(ref[z + 1, pl.ds(R0 + 8 * h, 8), :], q, 2 * z + h)
            return q

        xsend[f] = sweep(body, blank)

    load_k.wait()
    pack_planes(kb, ysendk, xsendk, 0)
    for f in range(NF):
        loads[f].wait()
        pack_planes(u0.at[f], ysend1, xsend1, f)
    for copy in small:
        copy.wait()
    pl.semaphore_wait(barrier, count)
    facesk.start()
    for face in faces1:
        face.start()
    greet(token.at[0])

    def sides(ref, z, h, yhalo, f, pack):
        row = R0 + 8 * h
        mid = ref[z + 1, pl.ds(row, 8), :]
        zm, zp = ref[z, pl.ds(row, 8), :], ref[z + 2, pl.ds(row, 8), :]
        ym, yp = ref[z + 1, pl.ds(row - 1, 8), :], ref[z + 1, pl.ds(row + 1, 8), :]
        if h == 0:
            ym = jnp.where(first_row, jnp.broadcast_to(yhalo[0, f, pl.ds(z, 1), :], (8, 128)), ym)
        else:
            yp = jnp.where(last_row, jnp.broadcast_to(yhalo[1, f, pl.ds(z, 1), :], (8, 128)), yp)
        edge = rolled(pack, lax.rem(128 - 2 * (2 * z + h), 128))
        xm = jnp.where(first_lane, edge, rolled(mid, 1))
        xp = jnp.where(last_lane, edge, rolled(mid, CX - 1))
        return mid, zm, zp, ym, yp, xm, xp

    facesk.wait_recv()
    kpack = halo_pack(xhalok, 0)

    def coefficients(z, carry):
        for h in range(2):
            at = pl.ds(8 * h, 8)
            mid, *others = sides(kb, z, h, yhalok, 0, kpack)
            means = [0.5 * (mid + w) for w in others]
            kz[z, at, :] = means[0]
            kz[z + 1, at, :] = means[1]
            for i in range(4):
                kf[i, z, at, :] = means[2 + i]
            kf[4, z, at, :] = 1.0 - ((means[0] + means[1]) + (means[2] + means[3]) + (means[4] + means[5]))
        return carry

    sweep(coefficients, 0)

    def advance(src, f, yhalo, xhalo, emit):
        pack = halo_pack(xhalo, f)
        cz, cy, cx = courant[0, f], courant[1, f], courant[2, f]
        total = cz + cy + cx

        def body(z, q):
            for h in range(2):
                at = pl.ds(8 * h, 8)
                mid, zm, zp, ym, yp, xm, xp = sides(src.at[f], z, h, yhalo, f, pack)
                value = (
                    (kf[4, z, at, :] - total) * mid
                    + (kz[z + 1, at, :] * zp + (kz[z, at, :] + cz) * zm)
                    + (kf[1, z, at, :] * yp + (kf[0, z, at, :] + cy) * ym)
                    + (kf[3, z, at, :] * xp + (kf[2, z, at, :] + cx) * xm)
                )
                emit(z, h, value)
                if q is not None:
                    q = packed(value, q, 2 * z + h)
            return q

        return body

    def step1(f):
        def emit(z, h, value):
            u1[f, z + 1, pl.ds(R0 + 8 * h, 8), :] = value
            side, row = (0, 0) if h == 0 else (1, 7)
            ysend2[side, f, pl.ds(z, 1), :] = value[row : row + 1, :]

        xsend2[f] = sweep(advance(u0, f, yhalo1, xhalo1, emit), blank)

    arrivals1 = {f: faces1[g] for g, (f, n) in enumerate(GROUPS1)}
    departures2 = {f + n - 1: faces2[g] for g, (f, n) in enumerate(GROUPS2)}
    for f in range(NF):
        if f in arrivals1:
            arrivals1[f].wait_recv()
        step1(f)
        if f in departures2:
            departures2[f].start()
    pl.semaphore_wait(token.at[0], 2)
    greet(token.at[1])

    def sites(z, h):
        start = h * 8 * CZ + lax.rem(z, 4) * 8 + lax.div(z, 4)
        return pl.ds(start, 8, stride=CZ)

    rs2, rm2 = rs.reshape(CY * CZ, CX), rm.reshape(CY * CZ, CX)
    rh2, rb2 = rh.reshape(CY * CZ, CX), rb.reshape(3, CY * CZ, CX)

    def step2(f):
        def emit(z, h, value):
            at = pl.ds(8 * h, 8)
            u2[f, z, at, :] = value
            if f == 0:
                sp[z + 1, pl.ds(R0 + 8 * h, 8), :] = value
                side, row = (0, 0) if h == 0 else (1, 7)
                ysend3[side, 0, pl.ds(z, 1), :] = value[row : row + 1, :]
                rs2[sites(z, h), :] = value
            elif f == 4:
                rm2[sites(z, h), :] = (-LOG2E) - (0.5 * LOG2E) * jnp.tanh(value)
            else:
                rb2[f - 1, sites(z, h), :] = 0.5 + 0.5 * jnp.tanh(0.5 * value)

        out = sweep(advance(u1, f, yhalo2, xhalo2, emit), blank if f == 0 else None)
        if f == 0:
            xsend3[0] = out

    arrivals2 = {f: faces2[g] for g, (f, n) in enumerate(GROUPS2)}
    for f in range(NF):
        if f in arrivals2:
            arrivals2[f].wait_recv()
        step2(f)
        if f == 0:
            faces3.start()

    faces3.wait_recv()
    spack = halo_pack(xhalo3, 0)

    def shading(z, carry):
        for h in range(2):
            _, zm, zp, ym, yp, xm, xp = sides(sp, z, h, yhalo3, 0, spack)
            gz, gy, gx = 0.5 * (zp - zm), 0.5 * (yp - ym), 0.5 * (xp - xm)
            shade = 0.35 + 0.65 * jnp.abs(0.64 * gz + 0.6 * gy + 0.48 * gx) * lax.rsqrt(
                gz * gz + gy * gy + gx * gx + 1.0
            )
            rh2[sites(z, h), :] = shade
        return carry

    sweep(shading, 0)
    pl.semaphore_wait(token.at[1], 2)

    pairs, relays = nz // 2, nz // 2 - 1
    odd = lax.rem(mes[0], 2)
    ahead = 2 * odd - 1
    mate = mes[0] - ahead
    mine = lax.div(mes[0], 2)

    def at_distance(start, d):
        return lax.rem(start + d * ahead + nz, nz)

    def block_copy(i, src, dst, z):
        return pltpu.make_async_remote_copy(
            src_ref=src, dst_ref=dst, send_sem=tile_send.at[i], recv_sem=tile_recv.at[i],
            device_id={"gz": z}, device_id_type=MESH,
        )

    def render(owner, dst):
        def tile(i, carry):
            p = perm[0, 0, owner * per_owner + i]
            t = lax.shift_right_logical(p, 4)
            y = lax.bitwise_and(p, 15)
            cover = mask[0, t, 0, y].astype(f32)
            mid, slope, amount = center[t], -LOG2E * sharp[t], gain[t]
            gap = rs[y] - mid
            depth = jnp.exp2(slope * (gap * gap)) * (amount * rm[y])
            e = [depth[0:8]]
            for w in range(1, 4):
                e.append(e[-1] + depth[8 * w : 8 * w + 8])
            inclusive = e[3]
            for sh in (1, 2, 4):
                inclusive = inclusive + jnp.where(sub >= sh, pltpu.roll(inclusive, sh, 0), 0.0)
            before = jnp.exp2(inclusive - e[3])
            lit = [jnp.exp2(x) for x in e]
            weight = [1.0 - lit[0]] + [lit[w] - lit[w + 1] for w in range(3)]
            shade = rh[y]
            weight = [weight[w] * shade[8 * w : 8 * w + 8] for w in range(4)]
            for k in range(3):
                base = rb[k, y]
                total = weight[0] * base[0:8]
                for w in range(1, 4):
                    total = total + weight[w] * base[8 * w : 8 * w + 8]
                total = jnp.sum(total * before, axis=0, keepdims=True)
                dst[k, pl.ds(i, 1), :] = total * (color[k, t] * cover)
            dst[3, pl.ds(i, 1), :] = (1.0 - jnp.exp2(inclusive[7:8])) * cover
            return carry

        lax.fori_loop(0, per_owner, tile, 0, unroll=8)

    def merge(theirs, own):
        for i in range(per_owner // 8):
            at = pl.ds(8 * i, 8)
            a = [theirs[k, at, :] for k in range(4)]
            b = [own[k, at, :] for k in range(4)]
            front = [jnp.where(odd == 1, x, y) for x, y in zip(a, b)]
            back = [jnp.where(odd == 1, y, x) for x, y in zip(a, b)]
            clear = 1.0 - front[3]
            for k in range(4):
                own[k, at, :] = front[k] + clear * back[k]

    def to_mate(d):
        return block_copy(pairs + d, mtiles.at[d - 1], mrecv.at[d - 1], mate)

    def onward(d):
        return pltpu.make_async_remote_copy(
            src_ref=rtiles.at[d - 1], dst_ref=recv.at[mine],
            send_sem=tile_send.at[d - 1], recv_sem=tile_recv.at[mine],
            device_id={"gz": at_distance(mes[0], d)}, device_id_type=MESH,
        )

    def pass_on(d):
        to_mate(d).wait_recv()
        merge(mrecv.at[d - 1], rtiles.at[d - 1])
        onward(d).start()

    order = list(range(relays, 0, -1))
    for d in order:
        render(at_distance(mate, -d), mtiles.at[d - 1])
        to_mate(d).start()
    pair_copy = block_copy(pairs, ptiles, precv, mate)
    for j, d in enumerate(order):
        render(at_distance(mes[0], d), rtiles.at[d - 1])
        if j:
            pass_on(order[j - 1])
    render(mate, ptiles)
    pair_copy.start()
    if order:
        pass_on(order[-1])
    render(mes[0], recv.at[mine])
    pair_copy.wait_recv()
    merge(precv, recv.at[mine])
    for o in range(1, pairs):
        q = lax.rem(mine + o, pairs)
        pltpu.make_async_remote_copy(
            src_ref=rtiles.at[0], dst_ref=recv.at[q], send_sem=tile_send.at[0], recv_sem=tile_recv.at[q],
            device_id={"gz": mate}, device_id_type=MESH,
        ).wait_recv()

    def composite(i, carry):
        at = pl.ds(pl.multiple_of(8 * i, 8), 8)
        acc = [recv[0, k, at, :] for k in range(4)]
        for s in range(1, pairs):
            clear = 1.0 - acc[3]
            acc = [acc[k] + clear * recv[s, k, at, :] for k in range(4)]
        for k in range(4):
            for r in range(8):
                pic_out[0, 0, 8 * i + r, pl.ds(k, 1), :] = acc[k][r : r + 1, :]
        return carry

    lax.fori_loop(0, per_owner // 8, composite, 0)
    for d in order:
        to_mate(d).wait_send()
        onward(d).wait_send()
    pair_copy.wait_send()
    for face in [facesk, *faces1, *faces2, faces3]:
        face.wait_send()


def flush(state, picture, state_out, picture_out, sem):
    copies = [pltpu.make_async_copy(picture, picture_out, sem.at[NF])]
    copies += [pltpu.make_async_copy(state.at[f], state_out.at[f], sem.at[f]) for f in range(NF)]
    for copy in copies:
        copy.start()
    for copy in copies:
        copy.wait()


def shards(fields, diffusivity, courant, tf_center, tf_sharp, tf_gain, tf_color, tile_mask, tile_perm):
    nz = lax.axis_size("gz")
    per_owner = TILES // nz
    f32 = jnp.float32
    vm = pltpu.VMEM
    anywhere = pl.BlockSpec(memory_space=pl.ANY)
    inside = pl.BlockSpec(memory_space=pltpu.VMEM)

    def halo(n):
        return [vm((2, n, CZ, CX), f32), vm((2, n, CZ, CX), f32), vm((n, 8, CX), f32), vm((2, n, 8, CX), f32)]

    sm = lambda a: pltpu.SMEM(a.shape, a.dtype)
    operands = (
        fields, diffusivity, courant.T, tf_center, tf_sharp, tf_gain, tf_color,
        jnp.transpose(tile_mask, (0, 1, 3, 2)), tile_perm,
    )
    results = pl.pallas_call(
        kernel,
        out_shape=(vm((NF, CZ, CY, CX), f32), vm((1, 1, per_owner, 4, CX), f32)),
        in_specs=[anywhere] * 9,
        out_specs=(inside, inside),
        scratch_shapes=[
            vm((CZ + 2, 32, CX), f32),
            vm((NF, CZ + 2, 32, CX), f32),
            vm((NF, CZ + 2, 32, CX), f32),
            vm((CZ + 2, 32, CX), f32),
            *halo(1), *halo(NF), *halo(NF), *halo(1),
            vm((CZ + 1, CY, CX), f32),
            vm((5, CZ, CY, CX), f32),
            vm((CY, CZ, CX), f32),
            vm((CY, CZ, CX), f32),
            vm((CY, CZ, CX), f32),
            vm((3, CY, CZ, CX), f32),
            *[vm((max(nz // 2 - 1, 1), 4, per_owner, CX), f32)] * 3,
            *[vm((4, per_owner, CX), f32)] * 2,
            vm((nz // 2, 4, per_owner, CX), f32),
            *[sm(a) for a in operands[2:]],
            pltpu.SemaphoreType.DMA((42,)),
            pltpu.SemaphoreType.DMA((42,)),
            pltpu.SemaphoreType.DMA((nz,)),
            pltpu.SemaphoreType.DMA((nz,)),
            pltpu.SemaphoreType.DMA((13,)),
            pltpu.SemaphoreType.REGULAR((2,)),
        ],
        compiler_params=pltpu.CompilerParams(collective_id=0, has_side_effects=True),
        name="insitu",
    )(*operands)
    return pl.pallas_call(
        flush,
        out_shape=tuple(jax.ShapeDtypeStruct(r.shape, f32) for r in results),
        in_specs=[inside] * 2,
        out_specs=(anywhere, anywhere),
        scratch_shapes=[pltpu.SemaphoreType.DMA((NF + 1,))],
        name="flush",
    )(*[pltpu.with_memory_space_constraint(r, pltpu.VMEM) for r in results])


def solution(mesh):
    return jax.shard_map(
        shards,
        mesh=mesh,
        in_specs=(
            P(None, "gz", "gy", "gx"),
            P("gz", "gy", "gx"),
            P(),
            P(),
            P(),
            P(),
            P(),
            P("gz", None, "gy", "gx"),
            P("gy", "gx", None),
        ),
        out_specs=(P(None, "gz", "gy", "gx"), P("gy", "gx", "gz", None, None)),
        check_vma=False,
    )
```

```python
import functools
import math

import jax
import jax.numpy as jnp
from jax import lax
from jax.experimental import pallas as pl
from jax.experimental.pallas import tpu as pltpu
from jax.sharding import PartitionSpec as P

MESH = pl.DeviceIdType.MESH
LOG2E = math.log2(math.e)
NF, CZ, CY, CX, TF = 5, 32, 16, 128, 16
R0 = 8
TILES = TF * CY
GROUPS1 = ((0, 2), (2, 3))
GROUPS2 = ((0, 1), (1, 2), (3, 2))
UNROLL = 32


def kernel(
    fields, kappa, courant_in, center_in, sharp_in, gain_in, color_in, mask_in, perm_in,
    u2, pic_out,
    kb, u0, u1, sp, ysendk, yhalok, xsendk, xhalok, ysend1, yhalo1, xsend1, xhalo1,
    ysend2, yhalo2, xsend2, xhalo2, ysend3, yhalo3, xsend3, xhalo3,
    kz, kf, rs, rm, rh, rb, mtiles, mrecv, rtiles, ptiles, precv, recv,
    courant, center, sharp, gain, color, mask, perm,
    send_sem, recv_sem, tile_send, tile_recv, local_sem, token,
):
    f32 = jnp.float32
    names = ("gz", "gy", "gx")
    sizes = [lax.axis_size(a) for a in names]
    mes = [lax.axis_index(a) for a in names]
    nz = sizes[0]
    per_owner = TILES // nz
    rows = pl.ds(R0, CY)

    def local(i, src, dst):
        copy = pltpu.make_async_copy(src, dst, local_sem.at[i])
        copy.start()
        return copy

    load_k = local(0, kappa, kb.at[pl.ds(1, CZ), rows, :])
    loads = [local(1 + f, fields.at[f], u0.at[f, pl.ds(1, CZ), rows, :]) for f in range(NF)]
    small = [
        local(6 + i, a, b)
        for i, (a, b) in enumerate(
            zip(
                (courant_in, center_in, sharp_in, gain_in, color_in, mask_in, perm_in),
                (courant, center, sharp, gain, color, mask, perm),
            )
        )
    ]

    def exists(a, side):
        return (mes[a] > 0) if side == 0 else (mes[a] < sizes[a] - 1)

    ring = [lax.rem(mes[0] + 1, nz), lax.rem(mes[0] + nz - 1, nz)]
    barrier = pltpu.get_barrier_semaphore()

    def greet(sem):
        for z in ring:
            pl.semaphore_signal(sem, inc=1, device_id={"gz": z}, device_id_type=MESH)

    greet(barrier)
    count = jnp.int32(2)
    for a in (1, 2):
        for side in (0, 1):
            ok = exists(a, side)

            @pl.when(ok)
            def _(a=a, side=side):
                pl.semaphore_signal(
                    barrier, inc=1, device_id={names[a]: mes[a] + 2 * side - 1}, device_id_type=MESH
                )

            count = count + ok.astype(jnp.int32)

    lane = lax.broadcasted_iota(jnp.int32, (8, 128), 1)
    sub = lax.broadcasted_iota(jnp.int32, (8, 128), 0)
    pair = lax.bitwise_and(lax.shift_right_logical(lane + 1, 1), 63)
    even = lax.bitwise_and(lane, 1) == 0
    first_lane, last_lane = lane == 0, lane == CX - 1
    first_row, last_row = sub == 0, sub == 7
    blank = jnp.zeros((8, 128), f32)

    def rolled(x, shift):
        return pltpu.roll(x, shift, 1)

    def packed(value, into, v):
        return jnp.where(pair == v, rolled(value, 2 * v), into)

    def halo_pack(ref, f):
        return jnp.where(even, rolled(ref[0, f], 1), rolled(ref[1, f], CX - 1))

    for a, side, refs in (
        (0, 0, (kb.at[0, rows, :], u0.at[:, 0, rows, :], u1.at[:, 0, rows, :], sp.at[0, rows, :])),
        (0, 1, (kb.at[CZ + 1, rows, :], u0.at[:, CZ + 1, rows, :], u1.at[:, CZ + 1, rows, :], sp.at[CZ + 1, rows, :])),
        *((1, s, tuple(r.at[s] for r in (yhalok, yhalo1, yhalo2, yhalo3))) for s in (0, 1)),
        *((2, s, tuple(r.at[s] for r in (xhalok, xhalo1, xhalo2, xhalo3))) for s in (0, 1)),
    ):

        @pl.when(jnp.logical_not(exists(a, side)))
        def _(refs=refs):
            for r in refs:
                r[...] = jnp.zeros(r.shape, f32)

    class Faces:
        def __init__(self, sem, parts):
            self.sem, self.parts = sem, parts

        def desc(self, a, side):
            src, dst = self.parts[2 * a + side]
            i = self.sem + 2 * a + side
            return pltpu.make_async_remote_copy(
                src_ref=src, dst_ref=dst, send_sem=send_sem.at[i], recv_sem=recv_sem.at[i],
                device_id={names[a]: mes[a] + 2 * side - 1}, device_id_type=MESH,
            )

        def each(self, what, incoming):
            for a in (1, 2, 0):
                for side in (0, 1):

                    @pl.when(exists(a, 1 - side if incoming else side))
                    def _(a=a, side=side):
                        getattr(self.desc(a, side), what)()

        def start(self):
            self.each("start", False)

        def wait_recv(self):
            self.each("wait_recv", True)

        def wait_send(self):
            self.each("wait_send", False)

    def yx_parts(ys, yh, xs, xh, at):
        return [
            (ys.at[0, at], yh.at[1, at]), (ys.at[1, at], yh.at[0, at]),
            (xs.at[at], xh.at[1, at]), (xs.at[at], xh.at[0, at]),
        ]

    one = pl.ds(0, 1)
    facesk = Faces(0, [
        (kappa.at[0], kb.at[CZ + 1, rows, :]), (kappa.at[CZ - 1], kb.at[0, rows, :]),
        *yx_parts(ysendk, yhalok, xsendk, xhalok, one),
    ])
    faces1, faces2 = [], []
    for g, (f, n) in enumerate(GROUPS1):
        at = pl.ds(f, n)
        faces1.append(Faces(6 + 6 * g, [
            (fields.at[at, 0], u0.at[at, CZ + 1, rows, :]), (fields.at[at, CZ - 1], u0.at[at, 0, rows, :]),
            *yx_parts(ysend1, yhalo1, xsend1, xhalo1, at),
        ]))
    for g, (f, n) in enumerate(GROUPS2):
        at = pl.ds(f, n)
        faces2.append(Faces(18 + 6 * g, [
            (u1.at[at, 1, rows, :], u1.at[at, CZ + 1, rows, :]), (u1.at[at, CZ, rows, :], u1.at[at, 0, rows, :]),
            *yx_parts(ysend2, yhalo2, xsend2, xhalo2, at),
        ]))
    faces3 = Faces(36, [
        (sp.at[1, rows, :], sp.at[CZ + 1, rows, :]), (sp.at[CZ, rows, :], sp.at[0, rows, :]),
        *yx_parts(ysend3, yhalo3, xsend3, xhalo3, one),
    ])

    def sweep(body, init):
        def step(i, carry):
            for j in range(UNROLL):
                carry = body(UNROLL * i + j, carry)
            return carry

        return lax.fori_loop(0, CZ // UNROLL, step, init)

    def pack_planes(ref, ysend, xsend, f):
        def body(z, q):
            ysend[0, f, pl.ds(z, 1), :] = ref[z + 1, pl.ds(R0, 1), :]
            ysend[1, f, pl.ds(z, 1), :] = ref[z + 1, pl.ds(R0 + CY - 1, 1), :]
            for h in range(2):
                q = packed(ref[z + 1, pl.ds(R0 + 8 * h, 8), :], q, 2 * z + h)
            return q

        xsend[f] = sweep(body, blank)

    load_k.wait()
    pack_planes(kb, ysendk, xsendk, 0)
    for f in range(NF):
        loads[f].wait()
        pack_planes(u0.at[f], ysend1, xsend1, f)
    pl.semaphore_wait(barrier, count)
    facesk.start()
    for face in faces1:
        face.start()
    greet(token.at[0])

    def sides(ref, z, h, yhalo, f, pack):
        row = R0 + 8 * h
        mid = ref[z + 1, pl.ds(row, 8), :]
        zm, zp = ref[z, pl.ds(row, 8), :], ref[z + 2, pl.ds(row, 8), :]
        ym, yp = ref[z + 1, pl.ds(row - 1, 8), :], ref[z + 1, pl.ds(row + 1, 8), :]
        if h == 0:
            ym = jnp.where(first_row, jnp.broadcast_to(yhalo[0, f, pl.ds(z, 1), :], (8, 128)), ym)
        else:
            yp = jnp.where(last_row, jnp.broadcast_to(yhalo[1, f, pl.ds(z, 1), :], (8, 128)), yp)
        edge = rolled(pack, lax.rem(128 - 2 * (2 * z + h), 128))
        xm = jnp.where(first_lane, edge, rolled(mid, 1))
        xp = jnp.where(last_lane, edge, rolled(mid, CX - 1))
        return mid, zm, zp, ym, yp, xm, xp

    facesk.wait_recv()
    kpack = halo_pack(xhalok, 0)

    def coefficients(z, carry):
        for h in range(2):
            at = pl.ds(8 * h, 8)
            mid, *others = sides(kb, z, h, yhalok, 0, kpack)
            means = [0.5 * (mid + w) for w in others]
            kz[z, at, :] = means[0]
            kz[z + 1, at, :] = means[1]
            for i in range(4):
                kf[i, z, at, :] = means[2 + i]
            kf[4, z, at, :] = 1.0 - ((means[0] + means[1]) + (means[2] + means[3]) + (means[4] + means[5]))
        return carry

    sweep(coefficients, 0)

    def advance(src, f, yhalo, xhalo, emit):
        pack = halo_pack(xhalo, f)
        cz, cy, cx = courant[0, f], courant[1, f], courant[2, f]
        total = cz + cy + cx

        def body(z, q):
            for h in range(2):
                at = pl.ds(8 * h, 8)
                mid, zm, zp, ym, yp, xm, xp = sides(src.at[f], z, h, yhalo, f, pack)
                value = (
                    (kf[4, z, at, :] - total) * mid
                    + (kz[z + 1, at, :] * zp + (kz[z, at, :] + cz) * zm)
                    + (kf[1, z, at, :] * yp + (kf[0, z, at, :] + cy) * ym)
                    + (kf[3, z, at, :] * xp + (kf[2, z, at, :] + cx) * xm)
                )
                emit(z, h, value)
                if q is not None:
                    q = packed(value, q, 2 * z + h)
            return q

        return body

    def step1(f):
        def emit(z, h, value):
            u1[f, z + 1, pl.ds(R0 + 8 * h, 8), :] = value
            side, row = (0, 0) if h == 0 else (1, 7)
            ysend2[side, f, pl.ds(z, 1), :] = value[row : row + 1, :]

        xsend2[f] = sweep(advance(u0, f, yhalo1, xhalo1, emit), blank)

    small[0].wait()
    arrivals1 = {f: faces1[g] for g, (f, n) in enumerate(GROUPS1)}
    departures2 = {f + n - 1: faces2[g] for g, (f, n) in enumerate(GROUPS2)}
    for f in range(NF):
        if f in arrivals1:
            arrivals1[f].wait_recv()
        step1(f)
        if f in departures2:
            departures2[f].start()
    pl.semaphore_wait(token.at[0], 2)
    greet(token.at[1])

    def sites(z, h):
        start = h * 8 * CZ + lax.rem(z, 4) * 8 + lax.div(z, 4)
        return pl.ds(start, 8, stride=CZ)

    rs2, rm2 = rs.reshape(CY * CZ, CX), rm.reshape(CY * CZ, CX)
    rh2, rb2 = rh.reshape(CY * CZ, CX), rb.reshape(3, CY * CZ, CX)

    def step2(f):
        def emit(z, h, value):
            at = pl.ds(8 * h, 8)
            u2[f, z, at, :] = value
            if f == 0:
                sp[z + 1, pl.ds(R0 + 8 * h, 8), :] = value
                side, row = (0, 0) if h == 0 else (1, 7)
                ysend3[side, 0, pl.ds(z, 1), :] = value[row : row + 1, :]
                rs2[sites(z, h), :] = value
            elif f == 4:
                rm2[sites(z, h), :] = (-LOG2E) - (0.5 * LOG2E) * jnp.tanh(value)
            else:
                rb2[f - 1, sites(z, h), :] = 0.5 + 0.5 * jnp.tanh(0.5 * value)

        out = sweep(advance(u1, f, yhalo2, xhalo2, emit), blank if f == 0 else None)
        if f == 0:
            xsend3[0] = out

    arrivals2 = {f: faces2[g] for g, (f, n) in enumerate(GROUPS2)}
    for f in range(NF):
        if f in arrivals2:
            arrivals2[f].wait_recv()
        step2(f)
        if f == 0:
            faces3.start()

    faces3.wait_recv()
    spack = halo_pack(xhalo3, 0)

    def shading(z, carry):
        for h in range(2):
            _, zm, zp, ym, yp, xm, xp = sides(sp, z, h, yhalo3, 0, spack)
            gz, gy, gx = 0.5 * (zp - zm), 0.5 * (yp - ym), 0.5 * (xp - xm)
            shade = 0.35 + 0.65 * jnp.abs(0.64 * gz + 0.6 * gy + 0.48 * gx) * lax.rsqrt(
                gz * gz + gy * gy + gx * gx + 1.0
            )
            rh2[sites(z, h), :] = shade
        return carry

    sweep(shading, 0)
    for copy in small[1:]:
        copy.wait()
    pl.semaphore_wait(token.at[1], 2)

    pairs, relays = nz // 2, nz // 2 - 1
    odd = lax.rem(mes[0], 2)
    ahead = 2 * odd - 1
    mate = mes[0] - ahead
    mine = lax.div(mes[0], 2)

    def at_distance(start, d):
        return lax.rem(start + d * ahead + nz, nz)

    def block_copy(i, src, dst, z):
        return pltpu.make_async_remote_copy(
            src_ref=src, dst_ref=dst, send_sem=tile_send.at[i], recv_sem=tile_recv.at[i],
            device_id={"gz": z}, device_id_type=MESH,
        )

    def gather_rows(x):
        low, mid, bit = sub < 4, lax.bitwise_and(sub, 2) == 0, lax.bitwise_and(sub, 1) == 0
        x = [
            jnp.where(low, x[i], x[i + 4]) + pltpu.roll(jnp.where(low, x[i + 4], x[i]), 4, 0)
            for i in range(4)
        ]
        for mask_, step in ((mid, 2), (bit, 1)):
            x = [
                jnp.where(
                    mask_, x[i] + pltpu.roll(x[i], 8 - step, 0), x[i + step] + pltpu.roll(x[i + step], step, 0)
                )
                for i in range(step)
            ]
        return x[0]

    def render(owner, dst):
        def eight(i8, carry):
            sums = [[], [], []]
            for j in range(8):
                i = 8 * i8 + j
                p = perm[0, 0, owner * per_owner + i]
                t = lax.shift_right_logical(p, 4)
                y = lax.bitwise_and(p, 15)
                cover = mask[0, t, 0, y].astype(f32)
                mid, slope, amount = center[t], -LOG2E * sharp[t], gain[t]
                gap = rs[y] - mid
                depth = jnp.exp2(slope * (gap * gap)) * (amount * rm[y])
                e = [depth[0:8]]
                for w in range(1, 4):
                    e.append(e[-1] + depth[8 * w : 8 * w + 8])
                inclusive = e[3]
                for sh in (1, 2, 4):
                    inclusive = inclusive + jnp.where(sub >= sh, pltpu.roll(inclusive, sh, 0), 0.0)
                before = jnp.exp2(inclusive - e[3])
                lit = [jnp.exp2(x) for x in e]
                weight = [1.0 - lit[0]] + [lit[w] - lit[w + 1] for w in range(3)]
                shade = rh[y]
                weight = [weight[w] * shade[8 * w : 8 * w + 8] for w in range(4)]
                for k in range(3):
                    base = rb[k, y]
                    total = weight[0] * base[0:8]
                    for w in range(1, 4):
                        total = total + weight[w] * base[8 * w : 8 * w + 8]
                    sums[k].append((total * before) * (color[k, t] * cover))
                dst[3, pl.ds(i, 1), :] = (1.0 - jnp.exp2(inclusive[7:8])) * cover
            for k in range(3):
                dst[k, pl.ds(pl.multiple_of(8 * i8, 8), 8), :] = gather_rows(sums[k])
            return carry

        lax.fori_loop(0, per_owner // 8, eight, 0)

    def merge(theirs, own):
        for i in range(per_owner // 8):
            at = pl.ds(8 * i, 8)
            a = [theirs[k, at, :] for k in range(4)]
            b = [own[k, at, :] for k in range(4)]
            front = [jnp.where(odd == 1, x, y) for x, y in zip(a, b)]
            back = [jnp.where(odd == 1, y, x) for x, y in zip(a, b)]
            clear = 1.0 - front[3]
            for k in range(4):
                own[k, at, :] = front[k] + clear * back[k]

    def to_mate(d):
        return block_copy(pairs + d, mtiles.at[d - 1], mrecv.at[d - 1], mate)

    def onward(d):
        return pltpu.make_async_remote_copy(
            src_ref=rtiles.at[d - 1], dst_ref=recv.at[mine],
            send_sem=tile_send.at[d - 1], recv_sem=tile_recv.at[mine],
            device_id={"gz": at_distance(mes[0], d)}, device_id_type=MESH,
        )

    def pass_on(d):
        to_mate(d).wait_recv()
        merge(mrecv.at[d - 1], rtiles.at[d - 1])
        onward(d).start()

    order = list(range(relays, 0, -1))
    for d in order:
        render(at_distance(mate, -d), mtiles.at[d - 1])
        to_mate(d).start()
    pair_copy = block_copy(pairs, ptiles, precv, mate)
    for j, d in enumerate(order):
        render(at_distance(mes[0], d), rtiles.at[d - 1])
        if j:
            pass_on(order[j - 1])
    render(mate, ptiles)
    pair_copy.start()
    if order:
        pass_on(order[-1])
    render(mes[0], recv.at[mine])
    pair_copy.wait_recv()
    merge(precv, recv.at[mine])
    for o in range(1, pairs):
        q = lax.rem(mine + o, pairs)
        pltpu.make_async_remote_copy(
            src_ref=rtiles.at[0], dst_ref=recv.at[q], send_sem=tile_send.at[0], recv_sem=tile_recv.at[q],
            device_id={"gz": mate}, device_id_type=MESH,
        ).wait_recv()

    def composite(i, carry):
        at = pl.ds(pl.multiple_of(8 * i, 8), 8)
        acc = [recv[0, k, at, :] for k in range(4)]
        for s in range(1, pairs):
            clear = 1.0 - acc[3]
            acc = [acc[k] + clear * recv[s, k, at, :] for k in range(4)]
        for k in range(4):
            for r in range(8):
                pic_out[0, 0, 8 * i + r, pl.ds(k, 1), :] = acc[k][r : r + 1, :]
        return carry

    lax.fori_loop(0, per_owner // 8, composite, 0)
    for d in order:
        to_mate(d).wait_send()
        onward(d).wait_send()
    pair_copy.wait_send()
    for face in [facesk, *faces1, *faces2, faces3]:
        face.wait_send()


def flush(state, picture, state_out, picture_out, sem):
    copies = [pltpu.make_async_copy(picture, picture_out, sem.at[NF])]
    copies += [pltpu.make_async_copy(state.at[f], state_out.at[f], sem.at[f]) for f in range(NF)]
    for copy in copies:
        copy.start()
    for copy in copies:
        copy.wait()


def shards(fields, diffusivity, courant, tf_center, tf_sharp, tf_gain, tf_color, tile_mask, tile_perm):
    nz = lax.axis_size("gz")
    per_owner = TILES // nz
    f32 = jnp.float32
    vm = pltpu.VMEM
    anywhere = pl.BlockSpec(memory_space=pl.ANY)
    inside = pl.BlockSpec(memory_space=pltpu.VMEM)

    def halo(n):
        return [vm((2, n, CZ, CX), f32), vm((2, n, CZ, CX), f32), vm((n, 8, CX), f32), vm((2, n, 8, CX), f32)]

    sm = lambda a: pltpu.SMEM(a.shape, a.dtype)
    operands = (
        fields, diffusivity, courant.T, tf_center, tf_sharp, tf_gain, tf_color,
        jnp.transpose(tile_mask, (0, 1, 3, 2)), tile_perm,
    )
    results = pl.pallas_call(
        kernel,
        out_shape=(vm((NF, CZ, CY, CX), f32), vm((1, 1, per_owner, 4, CX), f32)),
        in_specs=[anywhere] * 9,
        out_specs=(inside, inside),
        scratch_shapes=[
            vm((CZ + 2, 32, CX), f32),
            vm((NF, CZ + 2, 32, CX), f32),
            vm((NF, CZ + 2, 32, CX), f32),
            vm((CZ + 2, 32, CX), f32),
            *halo(1), *halo(NF), *halo(NF), *halo(1),
            vm((CZ + 1, CY, CX), f32),
            vm((5, CZ, CY, CX), f32),
            vm((CY, CZ, CX), f32),
            vm((CY, CZ, CX), f32),
            vm((CY, CZ, CX), f32),
            vm((3, CY, CZ, CX), f32),
            *[vm((max(nz // 2 - 1, 1), 4, per_owner, CX), f32)] * 3,
            *[vm((4, per_owner, CX), f32)] * 2,
            vm((nz // 2, 4, per_owner, CX), f32),
            *[sm(a) for a in operands[2:]],
            pltpu.SemaphoreType.DMA((42,)),
            pltpu.SemaphoreType.DMA((42,)),
            pltpu.SemaphoreType.DMA((nz,)),
            pltpu.SemaphoreType.DMA((nz,)),
            pltpu.SemaphoreType.DMA((13,)),
            pltpu.SemaphoreType.REGULAR((2,)),
        ],
        compiler_params=pltpu.CompilerParams(collective_id=0, has_side_effects=True),
        name="insitu",
    )(*operands)
    return pl.pallas_call(
        flush,
        out_shape=tuple(jax.ShapeDtypeStruct(r.shape, f32) for r in results),
        in_specs=[inside] * 2,
        out_specs=(anywhere, anywhere),
        scratch_shapes=[pltpu.SemaphoreType.DMA((NF + 1,))],
        name="flush",
    )(*[pltpu.with_memory_space_constraint(r, pltpu.VMEM) for r in results])


def solution(mesh):
    return jax.shard_map(
        shards,
        mesh=mesh,
        in_specs=(
            P(None, "gz", "gy", "gx"),
            P("gz", "gy", "gx"),
            P(),
            P(),
            P(),
            P(),
            P(),
            P("gz", None, "gy", "gx"),
            P("gy", "gx", None),
        ),
        out_specs=(P(None, "gz", "gy", "gx"), P("gy", "gx", "gz", None, None)),
        check_vma=False,
    )
```

```python
import functools
import math

import jax
import jax.numpy as jnp
from jax import lax
from jax.experimental import pallas as pl
from jax.experimental.pallas import tpu as pltpu
from jax.sharding import PartitionSpec as P

MESH = pl.DeviceIdType.MESH
LOG2E = math.log2(math.e)
NF, CZ, CY, CX, TF = 5, 32, 16, 128, 16
R0 = 8
TILES = TF * CY
GROUPS1 = ((0, 2), (2, 3))
GROUPS2 = ((0, 1), (1, 2), (3, 2))
UNROLL = 16


def kernel(
    fields, kappa, courant_in, center_in, sharp_in, gain_in, color_in, mask_in, perm_in,
    u2, pic_out,
    u0, u1, sp, ysend1, yhalo1, xsend1, xhalo1,
    ysend2, yhalo2, xsend2, xhalo2, ysend3, yhalo3, xsend3, xhalo3,
    kz, kf, rs, rh, rb, blocks, mrecv, precv, recv,
    courant, center, sharp, gain, color, mask, perm,
    send_sem, recv_sem, tile_send, tile_recv, local_sem, token,
):
    f32 = jnp.float32
    names = ("gz", "gy", "gx")
    sizes = [lax.axis_size(a) for a in names]
    mes = [lax.axis_index(a) for a in names]
    nz = sizes[0]
    per_owner = TILES // nz
    rows = pl.ds(R0, CY)

    def local(i, src, dst):
        copy = pltpu.make_async_copy(src, dst, local_sem.at[i])
        copy.start()
        return copy

    def load(f):
        return pltpu.make_async_copy(fields.at[f], u0.at[f, pl.ds(1, CZ), rows, :], local_sem.at[f])

    load_k = local(NF, kappa, u0.at[NF, pl.ds(1, CZ), rows, :])
    for f in range(NF):
        load(f).start()
    small = [
        local(NF + 1 + i, a, b)
        for i, (a, b) in enumerate(
            zip(
                (courant_in, center_in, sharp_in, gain_in, color_in, mask_in, perm_in),
                (courant, center, sharp, gain, color, mask, perm),
            )
        )
    ]

    def exists(a, side):
        return (mes[a] > 0) if side == 0 else (mes[a] < sizes[a] - 1)

    ring = [lax.rem(mes[0] + 1, nz), lax.rem(mes[0] + nz - 1, nz)]
    barrier = pltpu.get_barrier_semaphore()

    def greet(sem):
        for z in ring:
            pl.semaphore_signal(sem, inc=1, device_id={"gz": z}, device_id_type=MESH)

    greet(barrier)
    count = jnp.int32(2)
    for a in (1, 2):
        for side in (0, 1):
            ok = exists(a, side)

            @pl.when(ok)
            def _(a=a, side=side):
                pl.semaphore_signal(
                    barrier, inc=1, device_id={names[a]: mes[a] + 2 * side - 1}, device_id_type=MESH
                )

            count = count + ok.astype(jnp.int32)

    lane = lax.broadcasted_iota(jnp.int32, (8, 128), 1)
    sub = lax.broadcasted_iota(jnp.int32, (8, 128), 0)
    pair = lax.bitwise_and(lax.shift_right_logical(lane + 1, 1), 63)
    even = lax.bitwise_and(lane, 1) == 0
    first_lane, last_lane = lane == 0, lane == CX - 1
    first_row, last_row = sub == 0, sub == 7
    blank = jnp.zeros((8, 128), f32)

    def rolled(x, shift):
        return pltpu.roll(x, shift, 1)

    def packed(value, into, v):
        return jnp.where(pair == v, rolled(value, 2 * v), into)

    def halo_pack(ref, f):
        return jnp.where(even, rolled(ref[0, f], 1), rolled(ref[1, f], CX - 1))

    for a, side, refs in (
        (0, 0, (u0.at[:, 0, rows, :], u1.at[:, 0, rows, :], sp.at[0, rows, :])),
        (0, 1, (u0.at[:, CZ + 1, rows, :], u1.at[:, CZ + 1, rows, :], sp.at[CZ + 1, rows, :])),
        *((1, s, tuple(r.at[s] for r in (yhalo1, yhalo2, yhalo3))) for s in (0, 1)),
        *((2, s, tuple(r.at[s] for r in (xhalo1, xhalo2, xhalo3))) for s in (0, 1)),
    ):

        @pl.when(jnp.logical_not(exists(a, side)))
        def _(refs=refs):
            for r in refs:
                r[...] = jnp.zeros(r.shape, f32)

    class Faces:
        def __init__(self, sem, parts):
            self.sem, self.parts = sem, parts

        def desc(self, a, side):
            src, dst = self.parts[2 * a + side]
            i = self.sem + 2 * a + side
            return pltpu.make_async_remote_copy(
                src_ref=src, dst_ref=dst, send_sem=send_sem.at[i], recv_sem=recv_sem.at[i],
                device_id={names[a]: mes[a] + 2 * side - 1}, device_id_type=MESH,
            )

    def each(groups, what, incoming=False):
        for a in (1, 2, 0):
            for side in (0, 1):

                @pl.when(exists(a, 1 - side if incoming else side))
                def _(a=a, side=side):
                    for group in groups:
                        getattr(group.desc(a, side), what)()

    def yx_parts(ys, yh, xs, xh, at):
        return [
            (ys.at[0, at], yh.at[1, at]), (ys.at[1, at], yh.at[0, at]),
            (xs.at[at], xh.at[1, at]), (xs.at[at], xh.at[0, at]),
        ]

    one = pl.ds(0, 1)
    facesk = Faces(0, [
        (kappa.at[0], u0.at[NF, CZ + 1, rows, :]), (kappa.at[CZ - 1], u0.at[NF, 0, rows, :]),
        *yx_parts(ysend1, yhalo1, xsend1, xhalo1, pl.ds(NF, 1)),
    ])
    faces1, faces2 = [], []
    for g, (f, n) in enumerate(GROUPS1):
        at = pl.ds(f, n)
        faces1.append(Faces(6 + 6 * g, [
            (fields.at[at, 0], u0.at[at, CZ + 1, rows, :]), (fields.at[at, CZ - 1], u0.at[at, 0, rows, :]),
            *yx_parts(ysend1, yhalo1, xsend1, xhalo1, at),
        ]))
    for g, (f, n) in enumerate(GROUPS2):
        at = pl.ds(f, n)
        faces2.append(Faces(18 + 6 * g, [
            (u1.at[at, 1, rows, :], u1.at[at, CZ + 1, rows, :]), (u1.at[at, CZ, rows, :], u1.at[at, 0, rows, :]),
            *yx_parts(ysend2, yhalo2, xsend2, xhalo2, at),
        ]))
    faces3 = Faces(36, [
        (sp.at[1, rows, :], sp.at[CZ + 1, rows, :]), (sp.at[CZ, rows, :], sp.at[0, rows, :]),
        *yx_parts(ysend3, yhalo3, xsend3, xhalo3, one),
    ])

    def sweep(body, init):
        def step(i, carry):
            for j in range(UNROLL):
                carry = body(UNROLL * i + j, carry)
            return carry

        return lax.fori_loop(0, CZ // UNROLL, step, init)

    def pack_planes(f):
        ref = u0.at[f]

        def body(z, q):
            ysend1[0, f, pl.ds(z, 1), :] = ref[z + 1, pl.ds(R0, 1), :]
            ysend1[1, f, pl.ds(z, 1), :] = ref[z + 1, pl.ds(R0 + CY - 1, 1), :]
            for h in range(2):
                q = packed(ref[z + 1, pl.ds(R0 + 8 * h, 8), :], q, 2 * z + h)
            return q

        xsend1[f] = sweep(body, blank)

    load_k.wait()

    def pack_one(i, carry):
        @pl.when(i > 0)
        def _():
            load(i - 1).wait()

        pack_planes(lax.rem(i + NF, NF + 1))
        return carry

    lax.fori_loop(0, NF + 1, pack_one, 0)
    pl.semaphore_wait(barrier, count)
    each([facesk, *faces1], "start")
    greet(token.at[0])

    def sides(ref, z, h, yhalo, f, pack):
        row = R0 + 8 * h
        mid = ref[z + 1, pl.ds(row, 8), :]
        zm, zp = ref[z, pl.ds(row, 8), :], ref[z + 2, pl.ds(row, 8), :]
        ym, yp = ref[z + 1, pl.ds(row - 1, 8), :], ref[z + 1, pl.ds(row + 1, 8), :]
        if h == 0:
            ym = jnp.where(first_row, jnp.broadcast_to(yhalo[0, f, pl.ds(z, 1), :], (8, 128)), ym)
        else:
            yp = jnp.where(last_row, jnp.broadcast_to(yhalo[1, f, pl.ds(z, 1), :], (8, 128)), yp)
        edge = rolled(pack, lax.rem(128 - 2 * (2 * z + h), 128))
        xm = jnp.where(first_lane, edge, rolled(mid, 1))
        xp = jnp.where(last_lane, edge, rolled(mid, CX - 1))
        return mid, zm, zp, ym, yp, xm, xp

    each([facesk], "wait_recv", True)
    kpack = halo_pack(xhalo1, NF)

    def coefficients(z, carry):
        for h in range(2):
            at = pl.ds(8 * h, 8)
            mid, *others = sides(u0.at[NF], z, h, yhalo1, NF, kpack)
            means = [0.5 * (mid + w) for w in others]
            kz[z, at, :] = means[0]
            kz[z + 1, at, :] = means[1]
            for i in range(4):
                kf[i, z, at, :] = means[2 + i]
            kf[4, z, at, :] = 1.0 - ((means[0] + means[1]) + (means[2] + means[3]) + (means[4] + means[5]))
        return carry

    sweep(coefficients, 0)

    def advance(src, f, yhalo, xhalo, emit):
        pack = halo_pack(xhalo, f)
        cz, cy, cx = courant[0, f], courant[1, f], courant[2, f]
        total = cz + cy + cx

        def body(z, q):
            for h in range(2):
                at = pl.ds(8 * h, 8)
                mid, zm, zp, ym, yp, xm, xp = sides(src.at[f], z, h, yhalo, f, pack)
                value = (
                    (kf[4, z, at, :] - total) * mid
                    + (kz[z + 1, at, :] * zp + (kz[z, at, :] + cz) * zm)
                    + (kf[1, z, at, :] * yp + (kf[0, z, at, :] + cy) * ym)
                    + (kf[3, z, at, :] * xp + (kf[2, z, at, :] + cx) * xm)
                )
                emit(z, h, value)
                if q is not None:
                    q = packed(value, q, 2 * z + h)
            return q

        return body

    def step1(f):
        def emit(z, h, value):
            u1[f, z + 1, pl.ds(R0 + 8 * h, 8), :] = value
            side, row = (0, 0) if h == 0 else (1, 7)
            ysend2[side, f, pl.ds(z, 1), :] = value[row : row + 1, :]

        xsend2[f] = sweep(advance(u0, f, yhalo1, xhalo1, emit), blank)

    small[0].wait()

    def first(f, carry):
        for g, (f0, _) in enumerate(GROUPS1):

            @pl.when(f == f0)
            def _(g=g):
                each([faces1[g]], "wait_recv", True)

        step1(f)
        for g, (f0, n) in enumerate(GROUPS2):

            @pl.when(f == f0 + n - 1)
            def _(g=g):
                each([faces2[g]], "start")

        return carry

    lax.fori_loop(0, NF, first, 0)
    pl.semaphore_wait(token.at[0], 2)
    greet(token.at[1])

    def sites(z, h):
        start = h * 8 * CZ + lax.rem(z, 4) * 8 + lax.div(z, 4)
        return pl.ds(start, 8, stride=CZ)

    rs2, rh2 = rs.reshape(CY * CZ, CX), rh.reshape(CY * CZ, CX)
    rb2 = rb.reshape(4, CY * CZ, CX)

    def emit_scalar(z, h, value):
        u2[0, z, pl.ds(8 * h, 8), :] = value
        sp[z + 1, pl.ds(R0 + 8 * h, 8), :] = value
        side, row = (0, 0) if h == 0 else (1, 7)
        ysend3[side, 0, pl.ds(z, 1), :] = value[row : row + 1, :]
        rs2[sites(z, h), :] = value

    each([faces2[0]], "wait_recv", True)
    xsend3[0] = sweep(advance(u1, 0, yhalo2, xhalo2, emit_scalar), blank)
    each([faces3], "start")

    def second(f, carry):
        for g in (1, 2):

            @pl.when(f == GROUPS2[g][0])
            def _(g=g):
                each([faces2[g]], "wait_recv", True)

        last = f == NF - 1
        inner = jnp.where(last, 1.0, 0.5)
        outer = jnp.where(last, -0.5 * LOG2E, 0.5)
        base = jnp.where(last, -LOG2E, 0.5)

        def emit(z, h, value):
            u2[f, z, pl.ds(8 * h, 8), :] = value
            rb2[f - 1, sites(z, h), :] = base + outer * jnp.tanh(inner * value)

        sweep(advance(u1, f, yhalo2, xhalo2, emit), None)
        return carry

    lax.fori_loop(1, NF, second, 0)
    each([faces3], "wait_recv", True)
    spack = halo_pack(xhalo3, 0)

    def shading(z, carry):
        for h in range(2):
            _, zm, zp, ym, yp, xm, xp = sides(sp, z, h, yhalo3, 0, spack)
            gz, gy, gx = 0.5 * (zp - zm), 0.5 * (yp - ym), 0.5 * (xp - xm)
            shade = 0.35 + 0.65 * jnp.abs(0.64 * gz + 0.6 * gy + 0.48 * gx) * lax.rsqrt(
                gz * gz + gy * gy + gx * gx + 1.0
            )
            rh2[sites(z, h), :] = shade
        return carry

    sweep(shading, 0)
    for copy in small[1:]:
        copy.wait()
    pl.semaphore_wait(token.at[1], 2)

    pairs, relays = nz // 2, nz // 2 - 1
    odd = lax.rem(mes[0], 2)
    ahead = 2 * odd - 1
    mate = mes[0] - ahead
    mine = lax.div(mes[0], 2)

    def at_distance(start, d):
        return lax.rem(start + d * ahead + nz, nz)

    def block_copy(i, src, dst, z):
        return pltpu.make_async_remote_copy(
            src_ref=src, dst_ref=dst, send_sem=tile_send.at[i], recv_sem=tile_recv.at[i],
            device_id={"gz": z}, device_id_type=MESH,
        )

    def gather_rows(x):
        low, mid, bit = sub < 4, lax.bitwise_and(sub, 2) == 0, lax.bitwise_and(sub, 1) == 0
        x = [
            jnp.where(low, x[i], x[i + 4]) + pltpu.roll(jnp.where(low, x[i + 4], x[i]), 4, 0)
            for i in range(4)
        ]
        for mask_, step in ((mid, 2), (bit, 1)):
            x = [
                jnp.where(
                    mask_, x[i] + pltpu.roll(x[i], 8 - step, 0), x[i + step] + pltpu.roll(x[i + step], step, 0)
                )
                for i in range(step)
            ]
        return x[0]

    def render(owner, dst):
        def eight(i8, carry):
            sums = [[], [], []]
            for j in range(8):
                i = 8 * i8 + j
                p = perm[0, 0, owner * per_owner + i]
                t = lax.shift_right_logical(p, 4)
                y = lax.bitwise_and(p, 15)
                cover = mask[0, t, 0, y].astype(f32)
                mid, slope, amount = center[t], -LOG2E * sharp[t], gain[t]
                gap = rs[y] - mid
                depth = jnp.exp2(slope * (gap * gap)) * (amount * rb[3, y])
                e = [depth[0:8]]
                for w in range(1, 4):
                    e.append(e[-1] + depth[8 * w : 8 * w + 8])
                inclusive = e[3]
                for sh in (1, 2, 4):
                    inclusive = inclusive + jnp.where(sub >= sh, pltpu.roll(inclusive, sh, 0), 0.0)
                before = jnp.exp2(inclusive - e[3])
                lit = [jnp.exp2(x) for x in e]
                weight = [1.0 - lit[0]] + [lit[w] - lit[w + 1] for w in range(3)]
                shade = rh[y]
                weight = [weight[w] * shade[8 * w : 8 * w + 8] for w in range(4)]
                for k in range(3):
                    base = rb[k, y]
                    total = weight[0] * base[0:8]
                    for w in range(1, 4):
                        total = total + weight[w] * base[8 * w : 8 * w + 8]
                    sums[k].append((total * before) * (color[k, t] * cover))
                dst[3, pl.ds(i, 1), :] = (1.0 - jnp.exp2(inclusive[7:8])) * cover
            for k in range(3):
                dst[k, pl.ds(pl.multiple_of(8 * i8, 8), 8), :] = gather_rows(sums[k])
            return carry

        lax.fori_loop(0, per_owner // 8, eight, 0)

    def merge(theirs, own):
        def part(i, carry):
            at = pl.ds(pl.multiple_of(8 * i, 8), 8)
            a = [theirs[k, at, :] for k in range(4)]
            b = [own[k, at, :] for k in range(4)]
            front = [jnp.where(odd == 1, x, y) for x, y in zip(a, b)]
            back = [jnp.where(odd == 1, y, x) for x, y in zip(a, b)]
            clear = 1.0 - front[3]
            for k in range(4):
                own[k, at, :] = front[k] + clear * back[k]
            return carry

        lax.fori_loop(0, per_owner // 8, part, 0)

    def to_mate(k):
        return block_copy(pairs + 1 + k, blocks.at[k], mrecv.at[k], mate)

    def onward(k):
        return pltpu.make_async_remote_copy(
            src_ref=blocks.at[relays + k], dst_ref=recv.at[mine],
            send_sem=tile_send.at[k], recv_sem=tile_recv.at[mine],
            device_id={"gz": at_distance(mes[0], relays - k)}, device_id_type=MESH,
        )

    pair_copy = block_copy(pairs, blocks.at[2 * relays], precv, mate)

    def owner_step(k, carry):
        off = jnp.where(k < relays, k - relays - 1, jnp.where(k < 2 * relays, 2 * relays - k, k - 2 * relays - 1))
        render(at_distance(mes[0], off), blocks.at[k])

        @pl.when(k < relays)
        def _():
            to_mate(k).start()

        @pl.when(k == 2 * relays)
        def _():
            pair_copy.start()

        @pl.when(jnp.logical_and(k > relays, k <= 2 * relays))
        def _():
            r = k - relays - 1
            to_mate(r).wait_recv()
            merge(mrecv.at[r], blocks.at[relays + r])
            onward(r).start()

        return carry

    lax.fori_loop(0, nz, owner_step, 0)
    pair_copy.wait_recv()
    merge(precv, blocks.at[nz - 1])
    for o in range(1, pairs):
        q = lax.rem(mine + o, pairs)
        pltpu.make_async_remote_copy(
            src_ref=blocks.at[0], dst_ref=recv.at[q], send_sem=tile_send.at[0], recv_sem=tile_recv.at[q],
            device_id={"gz": mate}, device_id_type=MESH,
        ).wait_recv()

    def block_of(s, k, at):
        return jnp.where(mine == s, blocks[nz - 1, k, at, :], recv[s, k, at, :])

    def composite(i, carry):
        at = pl.ds(pl.multiple_of(8 * i, 8), 8)
        acc = [block_of(0, k, at) for k in range(4)]
        for s in range(1, pairs):
            clear = 1.0 - acc[3]
            acc = [acc[k] + clear * block_of(s, k, at) for k in range(4)]
        for k in range(4):
            for r in range(8):
                pic_out[0, 0, 8 * i + r, pl.ds(k, 1), :] = acc[k][r : r + 1, :]
        return carry

    lax.fori_loop(0, per_owner // 8, composite, 0)
    for k in range(relays):
        to_mate(k).wait_send()
        onward(k).wait_send()
    pair_copy.wait_send()
    each([facesk, *faces1, *faces2, faces3], "wait_send")


def flush(state, picture, state_out, picture_out, sem):
    copies = [pltpu.make_async_copy(picture, picture_out, sem.at[NF])]
    copies += [pltpu.make_async_copy(state.at[f], state_out.at[f], sem.at[f]) for f in range(NF)]
    for copy in copies:
        copy.start()
    for copy in copies:
        copy.wait()


def shards(fields, diffusivity, courant, tf_center, tf_sharp, tf_gain, tf_color, tile_mask, tile_perm):
    nz = lax.axis_size("gz")
    per_owner = TILES // nz
    f32 = jnp.float32
    vm = pltpu.VMEM
    anywhere = pl.BlockSpec(memory_space=pl.ANY)
    inside = pl.BlockSpec(memory_space=pltpu.VMEM)

    def halo(n):
        return [vm((2, n, CZ, CX), f32), vm((2, n, CZ, CX), f32), vm((n, 8, CX), f32), vm((2, n, 8, CX), f32)]

    sm = lambda a: pltpu.SMEM(a.shape, a.dtype)
    operands = (
        fields, diffusivity, courant.T, tf_center, tf_sharp, tf_gain, tf_color,
        jnp.transpose(tile_mask, (0, 1, 3, 2)), tile_perm,
    )
    results = pl.pallas_call(
        kernel,
        out_shape=(vm((NF, CZ, CY, CX), f32), vm((1, 1, per_owner, 4, CX), f32)),
        in_specs=[anywhere] * 9,
        out_specs=(inside, inside),
        scratch_shapes=[
            vm((NF + 1, CZ + 2, 32, CX), f32),
            vm((NF, CZ + 2, 32, CX), f32),
            vm((CZ + 2, 32, CX), f32),
            *halo(NF + 1), *halo(NF), *halo(1),
            vm((CZ + 1, CY, CX), f32),
            vm((5, CZ, CY, CX), f32),
            vm((CY, CZ, CX), f32),
            vm((CY, CZ, CX), f32),
            vm((4, CY, CZ, CX), f32),
            vm((nz, 4, per_owner, CX), f32),
            vm((max(nz // 2 - 1, 1), 4, per_owner, CX), f32),
            vm((4, per_owner, CX), f32),
            vm((nz // 2, 4, per_owner, CX), f32),
            *[sm(a) for a in operands[2:]],
            pltpu.SemaphoreType.DMA((42,)),
            pltpu.SemaphoreType.DMA((42,)),
            pltpu.SemaphoreType.DMA((nz,)),
            pltpu.SemaphoreType.DMA((nz,)),
            pltpu.SemaphoreType.DMA((13,)),
            pltpu.SemaphoreType.REGULAR((2,)),
        ],
        compiler_params=pltpu.CompilerParams(collective_id=0, has_side_effects=True),
        name="insitu",
    )(*operands)
    return pl.pallas_call(
        flush,
        out_shape=tuple(jax.ShapeDtypeStruct(r.shape, f32) for r in results),
        in_specs=[inside] * 2,
        out_specs=(anywhere, anywhere),
        scratch_shapes=[pltpu.SemaphoreType.DMA((NF + 1,))],
        name="flush",
    )(*[pltpu.with_memory_space_constraint(r, pltpu.VMEM) for r in results])


def solution(mesh):
    return jax.shard_map(
        shards,
        mesh=mesh,
        in_specs=(
            P(None, "gz", "gy", "gx"),
            P("gz", "gy", "gx"),
            P(),
            P(),
            P(),
            P(),
            P(),
            P("gz", None, "gy", "gx"),
            P("gy", "gx", None),
        ),
        out_specs=(P(None, "gz", "gy", "gx"), P("gy", "gx", "gz", None, None)),
        check_vma=False,
    )
```

```python
import functools
import math

import jax
import jax.numpy as jnp
from jax import lax
from jax.experimental import pallas as pl
from jax.experimental.pallas import tpu as pltpu
from jax.sharding import PartitionSpec as P

MESH = pl.DeviceIdType.MESH
LOG2E = math.log2(math.e)
NF, CZ, CY, CX, TF = 5, 32, 16, 128, 16
R0 = 8
TILES = TF * CY
GROUPS1 = ((0, 2), (2, 3))
GROUPS2 = ((0, 1), (1, 2), (3, 2))
UNROLL = 16


def kernel(
    fields, kappa, courant_in, center_in, sharp_in, gain_in, color_in, mask_in, perm_in,
    u2, pic_out,
    u0, u1, sp, ysend1, yhalo1, xsend1, xhalo1,
    ysend2, yhalo2, xsend2, xhalo2, ysend3, yhalo3, xsend3, xhalo3,
    kz, kf, rs, rh, rb, blocks, mrecv, precv, recv,
    courant, center, sharp, gain, color, mask, perm,
    send_sem, recv_sem, tile_send, tile_recv, local_sem, token,
):
    f32 = jnp.float32
    names = ("gz", "gy", "gx")
    sizes = [lax.axis_size(a) for a in names]
    mes = [lax.axis_index(a) for a in names]
    nz = sizes[0]
    per_owner = TILES // nz
    rows = pl.ds(R0, CY)

    def local(i, src, dst):
        copy = pltpu.make_async_copy(src, dst, local_sem.at[i])
        copy.start()
        return copy

    def load(f):
        return pltpu.make_async_copy(fields.at[f], u0.at[f, pl.ds(1, CZ), rows, :], local_sem.at[f])

    load_k = local(NF, kappa, u0.at[NF, pl.ds(1, CZ), rows, :])
    for f in range(NF):
        load(f).start()
    small = [
        local(NF + 1 + i, a, b)
        for i, (a, b) in enumerate(
            zip(
                (courant_in, center_in, sharp_in, gain_in, color_in, mask_in, perm_in),
                (courant, center, sharp, gain, color, mask, perm),
            )
        )
    ]

    def exists(a, side):
        return (mes[a] > 0) if side == 0 else (mes[a] < sizes[a] - 1)

    ring = [lax.rem(mes[0] + 1, nz), lax.rem(mes[0] + nz - 1, nz)]
    barrier = pltpu.get_barrier_semaphore()

    def greet(sem):
        for z in ring:
            pl.semaphore_signal(sem, inc=1, device_id={"gz": z}, device_id_type=MESH)

    greet(barrier)
    count = jnp.int32(2)
    for a in (1, 2):
        for side in (0, 1):
            ok = exists(a, side)

            @pl.when(ok)
            def _(a=a, side=side):
                pl.semaphore_signal(
                    barrier, inc=1, device_id={names[a]: mes[a] + 2 * side - 1}, device_id_type=MESH
                )

            count = count + ok.astype(jnp.int32)

    lane = lax.broadcasted_iota(jnp.int32, (8, 128), 1)
    sub = lax.broadcasted_iota(jnp.int32, (8, 128), 0)
    pair = lax.bitwise_and(lax.shift_right_logical(lane + 1, 1), 63)
    even = lax.bitwise_and(lane, 1) == 0
    first_lane, last_lane = lane == 0, lane == CX - 1
    first_row, last_row = sub == 0, sub == 7
    blank = jnp.zeros((8, 128), f32)

    def rolled(x, shift):
        return pltpu.roll(x, shift, 1)

    def wrap(shift):
        return shift % 128 if isinstance(shift, int) else lax.rem(shift, 128)

    def packed(value, into, v):
        return jnp.where(pair == v, rolled(value, 2 * v), into)

    def halo_pack(ref, f):
        return jnp.where(even, rolled(ref[0, f], 1), rolled(ref[1, f], CX - 1))

    for a, side, refs in (
        (0, 0, (u0.at[:, 0, rows, :], u1.at[:, 0, rows, :], sp.at[0, rows, :])),
        (0, 1, (u0.at[:, CZ + 1, rows, :], u1.at[:, CZ + 1, rows, :], sp.at[CZ + 1, rows, :])),
        *((1, s, tuple(r.at[s] for r in (yhalo1, yhalo2, yhalo3))) for s in (0, 1)),
        *((2, s, tuple(r.at[s] for r in (xhalo1, xhalo2, xhalo3))) for s in (0, 1)),
    ):

        @pl.when(jnp.logical_not(exists(a, side)))
        def _(refs=refs):
            for r in refs:
                r[...] = jnp.zeros(r.shape, f32)

    class Faces:
        def __init__(self, sem, parts):
            self.sem, self.parts = sem, parts

        def desc(self, a, side):
            src, dst = self.parts[2 * a + side]
            i = self.sem + 2 * a + side
            return pltpu.make_async_remote_copy(
                src_ref=src, dst_ref=dst, send_sem=send_sem.at[i], recv_sem=recv_sem.at[i],
                device_id={names[a]: mes[a] + 2 * side - 1}, device_id_type=MESH,
            )

    def each(groups, what, incoming=False):
        for a in (1, 2, 0):
            for side in (0, 1):

                @pl.when(exists(a, 1 - side if incoming else side))
                def _(a=a, side=side):
                    for group in groups:
                        getattr(group.desc(a, side), what)()

    def yx_parts(ys, yh, xs, xh, at):
        return [
            (ys.at[0, at], yh.at[1, at]), (ys.at[1, at], yh.at[0, at]),
            (xs.at[at], xh.at[1, at]), (xs.at[at], xh.at[0, at]),
        ]

    one = pl.ds(0, 1)
    facesk = Faces(0, [
        (kappa.at[0], u0.at[NF, CZ + 1, rows, :]), (kappa.at[CZ - 1], u0.at[NF, 0, rows, :]),
        *yx_parts(ysend1, yhalo1, xsend1, xhalo1, pl.ds(NF, 1)),
    ])
    faces1, faces2 = [], []
    for g, (f, n) in enumerate(GROUPS1):
        at = pl.ds(f, n)
        faces1.append(Faces(6 + 6 * g, [
            (fields.at[at, 0], u0.at[at, CZ + 1, rows, :]), (fields.at[at, CZ - 1], u0.at[at, 0, rows, :]),
            *yx_parts(ysend1, yhalo1, xsend1, xhalo1, at),
        ]))
    for g, (f, n) in enumerate(GROUPS2):
        at = pl.ds(f, n)
        faces2.append(Faces(18 + 6 * g, [
            (u1.at[at, 1, rows, :], u1.at[at, CZ + 1, rows, :]), (u1.at[at, CZ, rows, :], u1.at[at, 0, rows, :]),
            *yx_parts(ysend2, yhalo2, xsend2, xhalo2, at),
        ]))
    faces3 = Faces(36, [
        (sp.at[1, rows, :], sp.at[CZ + 1, rows, :]), (sp.at[CZ, rows, :], sp.at[0, rows, :]),
        *yx_parts(ysend3, yhalo3, xsend3, xhalo3, one),
    ])

    def sweep(body, init, unroll=CZ):
        def step(i, carry):
            for j in range(unroll):
                carry = body(unroll * i + j, carry)
            return carry

        if unroll == CZ:
            return step(0, init)
        return lax.fori_loop(0, CZ // unroll, step, init)

    def pack_planes(f):
        ref = u0.at[f]

        def body(z, q):
            ysend1[0, f, pl.ds(z, 1), :] = ref[z + 1, pl.ds(R0, 1), :]
            ysend1[1, f, pl.ds(z, 1), :] = ref[z + 1, pl.ds(R0 + CY - 1, 1), :]
            for h in range(2):
                q = packed(ref[z + 1, pl.ds(R0 + 8 * h, 8), :], q, 2 * z + h)
            return q

        xsend1[f] = sweep(body, blank)

    load_k.wait()

    def pack_one(i, carry):
        @pl.when(i > 0)
        def _():
            load(i - 1).wait()

        pack_planes(lax.rem(i + NF, NF + 1))

        @pl.when(i == 0)
        def _():
            pl.semaphore_wait(barrier, count)
            each([facesk], "start")

        for g, (f0, n) in enumerate(GROUPS1):

            @pl.when(i == f0 + n)
            def _(g=g):
                each([faces1[g]], "start")

        return carry

    lax.fori_loop(0, NF + 1, pack_one, 0)
    greet(token.at[0])

    def sides(ref, z, h, yhalo, f, pack):
        row = R0 + 8 * h
        mid = ref[z + 1, pl.ds(row, 8), :]
        zm, zp = ref[z, pl.ds(row, 8), :], ref[z + 2, pl.ds(row, 8), :]
        ym, yp = ref[z + 1, pl.ds(row - 1, 8), :], ref[z + 1, pl.ds(row + 1, 8), :]
        if h == 0:
            ym = jnp.where(first_row, jnp.broadcast_to(yhalo[0, f, pl.ds(z, 1), :], (8, 128)), ym)
        else:
            yp = jnp.where(last_row, jnp.broadcast_to(yhalo[1, f, pl.ds(z, 1), :], (8, 128)), yp)
        edge = rolled(pack, wrap(128 - 2 * (2 * z + h)))
        xm = jnp.where(first_lane, edge, rolled(mid, 1))
        xp = jnp.where(last_lane, edge, rolled(mid, CX - 1))
        return mid, zm, zp, ym, yp, xm, xp

    each([facesk], "wait_recv", True)
    kpack = halo_pack(xhalo1, NF)

    def coefficients(z, carry):
        for h in range(2):
            at = pl.ds(8 * h, 8)
            mid, *others = sides(u0.at[NF], z, h, yhalo1, NF, kpack)
            means = [0.5 * (mid + w) for w in others]
            kz[z, at, :] = means[0]
            kz[z + 1, at, :] = means[1]
            for i in range(4):
                kf[i, z, at, :] = means[2 + i]
            kf[4, z, at, :] = 1.0 - ((means[0] + means[1]) + (means[2] + means[3]) + (means[4] + means[5]))
        return carry

    sweep(coefficients, 0, UNROLL)

    def advance(src, f, yhalo, xhalo, emit):
        pack = halo_pack(xhalo, f)
        cz, cy, cx = courant[0, f], courant[1, f], courant[2, f]
        total = cz + cy + cx

        def body(z, q):
            for h in range(2):
                at = pl.ds(8 * h, 8)
                mid, zm, zp, ym, yp, xm, xp = sides(src.at[f], z, h, yhalo, f, pack)
                value = (
                    (kf[4, z, at, :] - total) * mid
                    + (kz[z + 1, at, :] * zp + (kz[z, at, :] + cz) * zm)
                    + (kf[1, z, at, :] * yp + (kf[0, z, at, :] + cy) * ym)
                    + (kf[3, z, at, :] * xp + (kf[2, z, at, :] + cx) * xm)
                )
                emit(z, h, value)
                if q is not None:
                    q = packed(value, q, 2 * z + h)
            return q

        return body

    def step1(f):
        def emit(z, h, value):
            u1[f, z + 1, pl.ds(R0 + 8 * h, 8), :] = value
            side, row = (0, 0) if h == 0 else (1, 7)
            ysend2[side, f, pl.ds(z, 1), :] = value[row : row + 1, :]

        xsend2[f] = sweep(advance(u0, f, yhalo1, xhalo1, emit), blank)

    small[0].wait()

    def first(f, carry):
        for g, (f0, _) in enumerate(GROUPS1):

            @pl.when(f == f0)
            def _(g=g):
                each([faces1[g]], "wait_recv", True)

        step1(f)
        for g, (f0, n) in enumerate(GROUPS2):

            @pl.when(f == f0 + n - 1)
            def _(g=g):
                each([faces2[g]], "start")

        return carry

    lax.fori_loop(0, NF, first, 0)
    pl.semaphore_wait(token.at[0], 2)
    greet(token.at[1])

    def sites(z, h):
        start = h * 8 * CZ + z % 4 * 8 + z // 4 if isinstance(z, int) else h * 8 * CZ + lax.rem(z, 4) * 8 + lax.div(z, 4)
        return pl.ds(start, 8, stride=CZ)

    rs2, rh2 = rs.reshape(CY * CZ, CX), rh.reshape(CY * CZ, CX)
    rb2 = rb.reshape(4, CY * CZ, CX)

    def emit_scalar(z, h, value):
        u2[0, z, pl.ds(8 * h, 8), :] = value
        sp[z + 1, pl.ds(R0 + 8 * h, 8), :] = value
        side, row = (0, 0) if h == 0 else (1, 7)
        ysend3[side, 0, pl.ds(z, 1), :] = value[row : row + 1, :]
        rs2[sites(z, h), :] = value

    each([faces2[0]], "wait_recv", True)
    xsend3[0] = sweep(advance(u1, 0, yhalo2, xhalo2, emit_scalar), blank, UNROLL)
    each([faces3], "start")

    def second(f, carry):
        for g in (1, 2):

            @pl.when(f == GROUPS2[g][0])
            def _(g=g):
                each([faces2[g]], "wait_recv", True)

        last = f == NF - 1
        inner = jnp.where(last, 1.0, 0.5)
        outer = jnp.where(last, -0.5 * LOG2E, 0.5)
        base = jnp.where(last, -LOG2E, 0.5)

        def emit(z, h, value):
            u2[f, z, pl.ds(8 * h, 8), :] = value
            rb2[f - 1, sites(z, h), :] = base + outer * jnp.tanh(inner * value)

        sweep(advance(u1, f, yhalo2, xhalo2, emit), None)
        return carry

    lax.fori_loop(1, NF, second, 0)
    each([faces3], "wait_recv", True)
    spack = halo_pack(xhalo3, 0)

    def shading(z, carry):
        for h in range(2):
            _, zm, zp, ym, yp, xm, xp = sides(sp, z, h, yhalo3, 0, spack)
            gz, gy, gx = 0.5 * (zp - zm), 0.5 * (yp - ym), 0.5 * (xp - xm)
            shade = 0.35 + 0.65 * jnp.abs(0.64 * gz + 0.6 * gy + 0.48 * gx) * lax.rsqrt(
                gz * gz + gy * gy + gx * gx + 1.0
            )
            rh2[sites(z, h), :] = shade
        return carry

    sweep(shading, 0, UNROLL)
    for copy in small[1:]:
        copy.wait()
    pl.semaphore_wait(token.at[1], 2)

    pairs, relays = nz // 2, nz // 2 - 1
    odd = lax.rem(mes[0], 2)
    ahead = 2 * odd - 1
    mate = mes[0] - ahead
    mine = lax.div(mes[0], 2)

    def at_distance(start, d):
        return lax.rem(start + d * ahead + nz, nz)

    def block_copy(i, src, dst, z):
        return pltpu.make_async_remote_copy(
            src_ref=src, dst_ref=dst, send_sem=tile_send.at[i], recv_sem=tile_recv.at[i],
            device_id={"gz": z}, device_id_type=MESH,
        )

    def render(owner, dst):
        def tile(i, carry):
            p = perm[0, 0, owner * per_owner + i]
            t = lax.shift_right_logical(p, 4)
            y = lax.bitwise_and(p, 15)
            cover = mask[0, t, 0, y].astype(f32)
            mid, slope, amount = center[t], -LOG2E * sharp[t], gain[t]
            gap = rs[y] - mid
            depth = jnp.exp2(slope * (gap * gap)) * (amount * rb[3, y])
            e = [depth[0:8]]
            for w in range(1, 4):
                e.append(e[-1] + depth[8 * w : 8 * w + 8])
            inclusive = e[3]
            for sh in (1, 2, 4):
                inclusive = inclusive + jnp.where(sub >= sh, pltpu.roll(inclusive, sh, 0), 0.0)
            before = jnp.exp2(inclusive - e[3])
            lit = [jnp.exp2(x) for x in e]
            weight = [1.0 - lit[0]] + [lit[w] - lit[w + 1] for w in range(3)]
            shade = rh[y]
            weight = [weight[w] * shade[8 * w : 8 * w + 8] for w in range(4)]
            for k in range(3):
                base = rb[k, y]
                total = weight[0] * base[0:8]
                for w in range(1, 4):
                    total = total + weight[w] * base[8 * w : 8 * w + 8]
                total = jnp.sum(total * before, axis=0, keepdims=True)
                dst[k, pl.ds(i, 1), :] = total * (color[k, t] * cover)
            dst[3, pl.ds(i, 1), :] = (1.0 - jnp.exp2(inclusive[7:8])) * cover
            return carry

        lax.fori_loop(0, per_owner, tile, 0, unroll=8)

    def merge(theirs, own):
        def part(i, carry):
            at = pl.ds(pl.multiple_of(8 * i, 8), 8)
            a = [theirs[k, at, :] for k in range(4)]
            b = [own[k, at, :] for k in range(4)]
            front = [jnp.where(odd == 1, x, y) for x, y in zip(a, b)]
            back = [jnp.where(odd == 1, y, x) for x, y in zip(a, b)]
            clear = 1.0 - front[3]
            for k in range(4):
                own[k, at, :] = front[k] + clear * back[k]
            return carry

        lax.fori_loop(0, per_owner // 8, part, 0)

    def to_mate(k):
        return block_copy(pairs + 1 + k, blocks.at[k], mrecv.at[k], mate)

    def onward(k):
        return pltpu.make_async_remote_copy(
            src_ref=blocks.at[relays + k], dst_ref=recv.at[mine],
            send_sem=tile_send.at[k], recv_sem=tile_recv.at[mine],
            device_id={"gz": at_distance(mes[0], relays - k)}, device_id_type=MESH,
        )

    pair_copy = block_copy(pairs, blocks.at[2 * relays], precv, mate)

    def owner_step(k, carry):
        off = jnp.where(k < relays, k - relays - 1, jnp.where(k < 2 * relays, 2 * relays - k, k - 2 * relays - 1))
        render(at_distance(mes[0], off), blocks.at[k])

        @pl.when(k < relays)
        def _():
            to_mate(k).start()

        @pl.when(k == 2 * relays)
        def _():
            pair_copy.start()

        @pl.when(jnp.logical_and(k > relays, k <= 2 * relays))
        def _():
            r = k - relays - 1
            to_mate(r).wait_recv()
            merge(mrecv.at[r], blocks.at[relays + r])
            onward(r).start()

        return carry

    lax.fori_loop(0, nz, owner_step, 0)
    pair_copy.wait_recv()
    merge(precv, blocks.at[nz - 1])
    for o in range(1, pairs):
        q = lax.rem(mine + o, pairs)
        pltpu.make_async_remote_copy(
            src_ref=blocks.at[0], dst_ref=recv.at[q], send_sem=tile_send.at[0], recv_sem=tile_recv.at[q],
            device_id={"gz": mate}, device_id_type=MESH,
        ).wait_recv()

    def block_of(s, k, at):
        return jnp.where(mine == s, blocks[nz - 1, k, at, :], recv[s, k, at, :])

    def composite(i, carry):
        at = pl.ds(pl.multiple_of(8 * i, 8), 8)
        acc = [block_of(0, k, at) for k in range(4)]
        for s in range(1, pairs):
            clear = 1.0 - acc[3]
            acc = [acc[k] + clear * block_of(s, k, at) for k in range(4)]
        for k in range(4):
            for r in range(8):
                pic_out[0, 0, 8 * i + r, pl.ds(k, 1), :] = acc[k][r : r + 1, :]
        return carry

    lax.fori_loop(0, per_owner // 8, composite, 0)
    for k in range(relays):
        to_mate(k).wait_send()
        onward(k).wait_send()
    pair_copy.wait_send()
    each([facesk, *faces1, *faces2, faces3], "wait_send")


def flush(state, picture, state_out, picture_out, sem):
    copies = [pltpu.make_async_copy(picture, picture_out, sem.at[NF])]
    copies += [pltpu.make_async_copy(state.at[f], state_out.at[f], sem.at[f]) for f in range(NF)]
    for copy in copies:
        copy.start()
    for copy in copies:
        copy.wait()


def shards(fields, diffusivity, courant, tf_center, tf_sharp, tf_gain, tf_color, tile_mask, tile_perm):
    nz = lax.axis_size("gz")
    per_owner = TILES // nz
    f32 = jnp.float32
    vm = pltpu.VMEM
    anywhere = pl.BlockSpec(memory_space=pl.ANY)
    inside = pl.BlockSpec(memory_space=pltpu.VMEM)

    def halo(n):
        return [vm((2, n, CZ, CX), f32), vm((2, n, CZ, CX), f32), vm((n, 8, CX), f32), vm((2, n, 8, CX), f32)]

    sm = lambda a: pltpu.SMEM(a.shape, a.dtype)
    operands = (
        fields, diffusivity, courant.T, tf_center, tf_sharp, tf_gain, tf_color,
        jnp.transpose(tile_mask, (0, 1, 3, 2)), tile_perm,
    )
    results = pl.pallas_call(
        kernel,
        out_shape=(vm((NF, CZ, CY, CX), f32), vm((1, 1, per_owner, 4, CX), f32)),
        in_specs=[anywhere] * 9,
        out_specs=(inside, inside),
        scratch_shapes=[
            vm((NF + 1, CZ + 2, 32, CX), f32),
            vm((NF, CZ + 2, 32, CX), f32),
            vm((CZ + 2, 32, CX), f32),
            *halo(NF + 1), *halo(NF), *halo(1),
            vm((CZ + 1, CY, CX), f32),
            vm((5, CZ, CY, CX), f32),
            vm((CY, CZ, CX), f32),
            vm((CY, CZ, CX), f32),
            vm((4, CY, CZ, CX), f32),
            vm((nz, 4, per_owner, CX), f32),
            vm((max(nz // 2 - 1, 1), 4, per_owner, CX), f32),
            vm((4, per_owner, CX), f32),
            vm((nz // 2, 4, per_owner, CX), f32),
            *[sm(a) for a in operands[2:]],
            pltpu.SemaphoreType.DMA((42,)),
            pltpu.SemaphoreType.DMA((42,)),
            pltpu.SemaphoreType.DMA((nz,)),
            pltpu.SemaphoreType.DMA((nz,)),
            pltpu.SemaphoreType.DMA((13,)),
            pltpu.SemaphoreType.REGULAR((2,)),
        ],
        compiler_params=pltpu.CompilerParams(collective_id=0, has_side_effects=True),
        name="insitu",
    )(*operands)
    return pl.pallas_call(
        flush,
        out_shape=tuple(jax.ShapeDtypeStruct(r.shape, f32) for r in results),
        in_specs=[inside] * 2,
        out_specs=(anywhere, anywhere),
        scratch_shapes=[pltpu.SemaphoreType.DMA((NF + 1,))],
        name="flush",
    )(*[pltpu.with_memory_space_constraint(r, pltpu.VMEM) for r in results])


def solution(mesh):
    return jax.shard_map(
        shards,
        mesh=mesh,
        in_specs=(
            P(None, "gz", "gy", "gx"),
            P("gz", "gy", "gx"),
            P(),
            P(),
            P(),
            P(),
            P(),
            P("gz", None, "gy", "gx"),
            P("gy", "gx", None),
        ),
        out_specs=(P(None, "gz", "gy", "gx"), P("gy", "gx", "gz", None, None)),
        check_vma=False,
    )
```

```python
import functools
import math

import jax
import jax.numpy as jnp
from jax import lax
from jax.experimental import pallas as pl
from jax.experimental.pallas import tpu as pltpu
from jax.sharding import PartitionSpec as P

MESH = pl.DeviceIdType.MESH
LOG2E = math.log2(math.e)
NF, CZ, CY, CX, TF = 5, 32, 16, 128, 16
R0 = 8
TILES = TF * CY
GROUPS1 = ((0, 1), (1, 1), (2, 1), (3, 1), (4, 1))
GROUPS2 = ((0, 1), (1, 1), (2, 1), (3, 1), (4, 1))
UNROLL = 16


def kernel(
    fields, kappa, courant_in, center_in, sharp_in, gain_in, color_in, mask_in, perm_in,
    u2, pic_out,
    kb, u0, u1, sp, ysendk, yhalok, xsendk, xhalok, ysend1, yhalo1, xsend1, xhalo1,
    ysend2, yhalo2, xsend2, xhalo2, ysend3, yhalo3, xsend3, xhalo3,
    kz, kf, rs, rm, rh, rb, mtiles, mrecv, rtiles, ptiles, precv, recv,
    courant, center, sharp, gain, color, mask, perm,
    send_sem, recv_sem, tile_send, tile_recv, local_sem, token,
):
    f32 = jnp.float32
    names = ("gz", "gy", "gx")
    sizes = [lax.axis_size(a) for a in names]
    mes = [lax.axis_index(a) for a in names]
    nz = sizes[0]
    per_owner = TILES // nz
    rows = pl.ds(R0, CY)

    def local(i, src, dst):
        copy = pltpu.make_async_copy(src, dst, local_sem.at[i])
        copy.start()
        return copy

    load_k = local(0, kappa, kb.at[pl.ds(1, CZ), rows, :])
    loads = [local(1 + f, fields.at[f], u0.at[f, pl.ds(1, CZ), rows, :]) for f in range(NF)]
    small = [
        local(6 + i, a, b)
        for i, (a, b) in enumerate(
            zip(
                (courant_in, center_in, sharp_in, gain_in, color_in, mask_in, perm_in),
                (courant, center, sharp, gain, color, mask, perm),
            )
        )
    ]

    def exists(a, side):
        return (mes[a] > 0) if side == 0 else (mes[a] < sizes[a] - 1)

    ring = [lax.rem(mes[0] + 1, nz), lax.rem(mes[0] + nz - 1, nz)]
    barrier = pltpu.get_barrier_semaphore()

    def greet(sem):
        for z in ring:
            pl.semaphore_signal(sem, inc=1, device_id={"gz": z}, device_id_type=MESH)

    greet(barrier)
    count = jnp.int32(2)
    for a in (1, 2):
        for side in (0, 1):
            ok = exists(a, side)

            @pl.when(ok)
            def _(a=a, side=side):
                pl.semaphore_signal(
                    barrier, inc=1, device_id={names[a]: mes[a] + 2 * side - 1}, device_id_type=MESH
                )

            count = count + ok.astype(jnp.int32)

    lane = lax.broadcasted_iota(jnp.int32, (8, 128), 1)
    sub = lax.broadcasted_iota(jnp.int32, (8, 128), 0)
    pair = lax.bitwise_and(lax.shift_right_logical(lane + 1, 1), 63)
    even = lax.bitwise_and(lane, 1) == 0
    first_lane, last_lane = lane == 0, lane == CX - 1
    first_row, last_row = sub == 0, sub == 7
    blank = jnp.zeros((8, 128), f32)

    def rolled(x, shift):
        return pltpu.roll(x, shift, 1)

    def packed(value, into, v):
        return jnp.where(pair == v, rolled(value, 2 * v), into)

    def halo_pack(ref, f):
        return jnp.where(even, rolled(ref[0, f], 1), rolled(ref[1, f], CX - 1))

    for a, side, refs in (
        (0, 0, (kb.at[0, rows, :], u0.at[:, 0, rows, :], u1.at[:, 0, rows, :], sp.at[0, rows, :])),
        (0, 1, (kb.at[CZ + 1, rows, :], u0.at[:, CZ + 1, rows, :], u1.at[:, CZ + 1, rows, :], sp.at[CZ + 1, rows, :])),
        *((1, s, tuple(r.at[s] for r in (yhalok, yhalo1, yhalo2, yhalo3))) for s in (0, 1)),
        *((2, s, tuple(r.at[s] for r in (xhalok, xhalo1, xhalo2, xhalo3))) for s in (0, 1)),
    ):

        @pl.when(jnp.logical_not(exists(a, side)))
        def _(refs=refs):
            for r in refs:
                r[...] = jnp.zeros(r.shape, f32)

    class Faces:
        def __init__(self, sem, parts):
            self.sem, self.parts = sem, parts

        def desc(self, a, side):
            src, dst = self.parts[2 * a + side]
            i = self.sem + 2 * a + side
            return pltpu.make_async_remote_copy(
                src_ref=src, dst_ref=dst, send_sem=send_sem.at[i], recv_sem=recv_sem.at[i],
                device_id={names[a]: mes[a] + 2 * side - 1}, device_id_type=MESH,
            )

        def each(self, what, incoming):
            for a in (1, 2, 0):
                for side in (0, 1):

                    @pl.when(exists(a, 1 - side if incoming else side))
                    def _(a=a, side=side):
                        getattr(self.desc(a, side), what)()

        def start(self):
            self.each("start", False)

        def wait_recv(self):
            self.each("wait_recv", True)

        def wait_send(self):
            self.each("wait_send", False)

    def yx_parts(ys, yh, xs, xh, at):
        return [
            (ys.at[0, at], yh.at[1, at]), (ys.at[1, at], yh.at[0, at]),
            (xs.at[at], xh.at[1, at]), (xs.at[at], xh.at[0, at]),
        ]

    one = pl.ds(0, 1)
    facesk = Faces(0, [
        (kappa.at[0], kb.at[CZ + 1, rows, :]), (kappa.at[CZ - 1], kb.at[0, rows, :]),
        *yx_parts(ysendk, yhalok, xsendk, xhalok, one),
    ])
    faces1, faces2 = [], []
    for g, (f, n) in enumerate(GROUPS1):
        at = pl.ds(f, n)
        faces1.append(Faces(6 + 6 * g, [
            (fields.at[at, 0], u0.at[at, CZ + 1, rows, :]), (fields.at[at, CZ - 1], u0.at[at, 0, rows, :]),
            *yx_parts(ysend1, yhalo1, xsend1, xhalo1, at),
        ]))
    for g, (f, n) in enumerate(GROUPS2):
        at = pl.ds(f, n)
        faces2.append(Faces(36 + 6 * g, [
            (u1.at[at, 1, rows, :], u1.at[at, CZ + 1, rows, :]), (u1.at[at, CZ, rows, :], u1.at[at, 0, rows, :]),
            *yx_parts(ysend2, yhalo2, xsend2, xhalo2, at),
        ]))
    faces3 = Faces(66, [
        (sp.at[1, rows, :], sp.at[CZ + 1, rows, :]), (sp.at[CZ, rows, :], sp.at[0, rows, :]),
        *yx_parts(ysend3, yhalo3, xsend3, xhalo3, one),
    ])

    def sweep(body, init):
        def step(i, carry):
            for j in range(UNROLL):
                carry = body(UNROLL * i + j, carry)
            return carry

        return lax.fori_loop(0, CZ // UNROLL, step, init)

    def pack_planes(ref, ysend, xsend, f):
        def body(z, q):
            ysend[0, f, pl.ds(z, 1), :] = ref[z + 1, pl.ds(R0, 1), :]
            ysend[1, f, pl.ds(z, 1), :] = ref[z + 1, pl.ds(R0 + CY - 1, 1), :]
            for h in range(2):
                q = packed(ref[z + 1, pl.ds(R0 + 8 * h, 8), :], q, 2 * z + h)
            return q

        xsend[f] = sweep(body, blank)

    load_k.wait()
    pack_planes(kb, ysendk, xsendk, 0)
    pl.semaphore_wait(barrier, count)
    facesk.start()
    for f in range(NF):
        loads[f].wait()
        pack_planes(u0.at[f], ysend1, xsend1, f)
        for g, (f0, n) in enumerate(GROUPS1):
            if f == f0 + n - 1:
                faces1[g].start()
    for copy in small:
        copy.wait()
    greet(token.at[0])

    def sides(ref, z, h, yhalo, f, pack):
        row = R0 + 8 * h
        mid = ref[z + 1, pl.ds(row, 8), :]
        zm, zp = ref[z, pl.ds(row, 8), :], ref[z + 2, pl.ds(row, 8), :]
        ym, yp = ref[z + 1, pl.ds(row - 1, 8), :], ref[z + 1, pl.ds(row + 1, 8), :]
        if h == 0:
            ym = jnp.where(first_row, jnp.broadcast_to(yhalo[0, f, pl.ds(z, 1), :], (8, 128)), ym)
        else:
            yp = jnp.where(last_row, jnp.broadcast_to(yhalo[1, f, pl.ds(z, 1), :], (8, 128)), yp)
        edge = rolled(pack, lax.rem(128 - 2 * (2 * z + h), 128))
        xm = jnp.where(first_lane, edge, rolled(mid, 1))
        xp = jnp.where(last_lane, edge, rolled(mid, CX - 1))
        return mid, zm, zp, ym, yp, xm, xp

    facesk.wait_recv()
    kpack = halo_pack(xhalok, 0)

    def coefficients(z, carry):
        for h in range(2):
            at = pl.ds(8 * h, 8)
            mid, *others = sides(kb, z, h, yhalok, 0, kpack)
            means = [0.5 * (mid + w) for w in others]
            kz[z, at, :] = means[0]
            kz[z + 1, at, :] = means[1]
            for i in range(4):
                kf[i, z, at, :] = means[2 + i]
            kf[4, z, at, :] = 1.0 - ((means[0] + means[1]) + (means[2] + means[3]) + (means[4] + means[5]))
        return carry

    sweep(coefficients, 0)

    def advance(src, f, yhalo, xhalo, emit):
        pack = halo_pack(xhalo, f)
        cz, cy, cx = courant[0, f], courant[1, f], courant[2, f]
        total = cz + cy + cx

        def body(z, q):
            for h in range(2):
                at = pl.ds(8 * h, 8)
                mid, zm, zp, ym, yp, xm, xp = sides(src.at[f], z, h, yhalo, f, pack)
                value = (
                    (kf[4, z, at, :] - total) * mid
                    + (kz[z + 1, at, :] * zp + (kz[z, at, :] + cz) * zm)
                    + (kf[1, z, at, :] * yp + (kf[0, z, at, :] + cy) * ym)
                    + (kf[3, z, at, :] * xp + (kf[2, z, at, :] + cx) * xm)
                )
                emit(z, h, value)
                if q is not None:
                    q = packed(value, q, 2 * z + h)
            return q

        return body

    def step1(f):
        def emit(z, h, value):
            u1[f, z + 1, pl.ds(R0 + 8 * h, 8), :] = value
            side, row = (0, 0) if h == 0 else (1, 7)
            ysend2[side, f, pl.ds(z, 1), :] = value[row : row + 1, :]

        xsend2[f] = sweep(advance(u0, f, yhalo1, xhalo1, emit), blank)

    arrivals1 = {f: faces1[g] for g, (f, n) in enumerate(GROUPS1)}
    departures2 = {f + n - 1: faces2[g] for g, (f, n) in enumerate(GROUPS2)}
    for f in range(NF):
        if f in arrivals1:
            arrivals1[f].wait_recv()
        step1(f)
        if f in departures2:
            departures2[f].start()
    pl.semaphore_wait(token.at[0], 2)
    greet(token.at[1])

    def sites(z, h):
        start = h * 8 * CZ + lax.rem(z, 4) * 8 + lax.div(z, 4)
        return pl.ds(start, 8, stride=CZ)

    rs2, rm2 = rs.reshape(CY * CZ, CX), rm.reshape(CY * CZ, CX)
    rh2, rb2 = rh.reshape(CY * CZ, CX), rb.reshape(3, CY * CZ, CX)

    def step2(f):
        def emit(z, h, value):
            at = pl.ds(8 * h, 8)
            u2[f, z, at, :] = value
            if f == 0:
                sp[z + 1, pl.ds(R0 + 8 * h, 8), :] = value
                side, row = (0, 0) if h == 0 else (1, 7)
                ysend3[side, 0, pl.ds(z, 1), :] = value[row : row + 1, :]
                rs2[sites(z, h), :] = value
            elif f == 4:
                rm2[sites(z, h), :] = (-LOG2E) - (0.5 * LOG2E) * jnp.tanh(value)
            else:
                rb2[f - 1, sites(z, h), :] = 0.5 + 0.5 * jnp.tanh(0.5 * value)

        out = sweep(advance(u1, f, yhalo2, xhalo2, emit), blank if f == 0 else None)
        if f == 0:
            xsend3[0] = out

    arrivals2 = {f: faces2[g] for g, (f, n) in enumerate(GROUPS2)}
    for f in range(NF):
        if f in arrivals2:
            arrivals2[f].wait_recv()
        step2(f)
        if f == 0:
            faces3.start()

    faces3.wait_recv()
    spack = halo_pack(xhalo3, 0)

    def shading(z, carry):
        for h in range(2):
            _, zm, zp, ym, yp, xm, xp = sides(sp, z, h, yhalo3, 0, spack)
            gz, gy, gx = 0.5 * (zp - zm), 0.5 * (yp - ym), 0.5 * (xp - xm)
            shade = 0.35 + 0.65 * jnp.abs(0.64 * gz + 0.6 * gy + 0.48 * gx) * lax.rsqrt(
                gz * gz + gy * gy + gx * gx + 1.0
            )
            rh2[sites(z, h), :] = shade
        return carry

    sweep(shading, 0)
    pl.semaphore_wait(token.at[1], 2)

    pairs, relays = nz // 2, nz // 2 - 1
    odd = lax.rem(mes[0], 2)
    ahead = 2 * odd - 1
    mate = mes[0] - ahead
    mine = lax.div(mes[0], 2)

    def at_distance(start, d):
        return lax.rem(start + d * ahead + nz, nz)

    def block_copy(i, src, dst, z):
        return pltpu.make_async_remote_copy(
            src_ref=src, dst_ref=dst, send_sem=tile_send.at[i], recv_sem=tile_recv.at[i],
            device_id={"gz": z}, device_id_type=MESH,
        )

    def render(owner, dst):
        def tile(i, carry):
            p = perm[0, 0, owner * per_owner + i]
            t = lax.shift_right_logical(p, 4)
            y = lax.bitwise_and(p, 15)
            cover = mask[0, t, 0, y].astype(f32)
            mid, slope, amount = center[t], -LOG2E * sharp[t], gain[t]
            gap = rs[y] - mid
            depth = jnp.exp2(slope * (gap * gap)) * (amount * rm[y])
            e = [depth[0:8]]
            for w in range(1, 4):
                e.append(e[-1] + depth[8 * w : 8 * w + 8])
            inclusive = e[3]
            for sh in (1, 2, 4):
                inclusive = inclusive + jnp.where(sub >= sh, pltpu.roll(inclusive, sh, 0), 0.0)
            before = jnp.exp2(inclusive - e[3])
            lit = [jnp.exp2(x) for x in e]
            weight = [1.0 - lit[0]] + [lit[w] - lit[w + 1] for w in range(3)]
            shade = rh[y]
            weight = [weight[w] * shade[8 * w : 8 * w + 8] for w in range(4)]
            for k in range(3):
                base = rb[k, y]
                total = weight[0] * base[0:8]
                for w in range(1, 4):
                    total = total + weight[w] * base[8 * w : 8 * w + 8]
                total = jnp.sum(total * before, axis=0, keepdims=True)
                dst[k, pl.ds(i, 1), :] = total * (color[k, t] * cover)
            dst[3, pl.ds(i, 1), :] = (1.0 - jnp.exp2(inclusive[7:8])) * cover
            return carry

        lax.fori_loop(0, per_owner, tile, 0, unroll=4)

    def merge(theirs, own):
        for i in range(per_owner // 8):
            at = pl.ds(8 * i, 8)
            a = [theirs[k, at, :] for k in range(4)]
            b = [own[k, at, :] for k in range(4)]
            front = [jnp.where(odd == 1, x, y) for x, y in zip(a, b)]
            back = [jnp.where(odd == 1, y, x) for x, y in zip(a, b)]
            clear = 1.0 - front[3]
            for k in range(4):
                own[k, at, :] = front[k] + clear * back[k]

    def to_mate(d):
        return block_copy(pairs + d, mtiles.at[d - 1], mrecv.at[d - 1], mate)

    def onward(d):
        return pltpu.make_async_remote_copy(
            src_ref=rtiles.at[d - 1], dst_ref=recv.at[mine],
            send_sem=tile_send.at[d - 1], recv_sem=tile_recv.at[mine],
            device_id={"gz": at_distance(mes[0], d)}, device_id_type=MESH,
        )

    def pass_on(d):
        to_mate(d).wait_recv()
        merge(mrecv.at[d - 1], rtiles.at[d - 1])
        onward(d).start()

    order = list(range(relays, 0, -1))
    for d in order:
        render(at_distance(mate, -d), mtiles.at[d - 1])
        to_mate(d).start()
    pair_copy = block_copy(pairs, ptiles, precv, mate)
    for j, d in enumerate(order):
        render(at_distance(mes[0], d), rtiles.at[d - 1])
        if j:
            pass_on(order[j - 1])
    render(mate, ptiles)
    pair_copy.start()
    if order:
        pass_on(order[-1])
    render(mes[0], recv.at[mine])
    pair_copy.wait_recv()
    merge(precv, recv.at[mine])
    for o in range(1, pairs):
        q = lax.rem(mine + o, pairs)
        pltpu.make_async_remote_copy(
            src_ref=rtiles.at[0], dst_ref=recv.at[q], send_sem=tile_send.at[0], recv_sem=tile_recv.at[q],
            device_id={"gz": mate}, device_id_type=MESH,
        ).wait_recv()

    def composite(i, carry):
        at = pl.ds(pl.multiple_of(8 * i, 8), 8)
        acc = [recv[0, k, at, :] for k in range(4)]
        for s in range(1, pairs):
            clear = 1.0 - acc[3]
            acc = [acc[k] + clear * recv[s, k, at, :] for k in range(4)]
        for k in range(4):
            for r in range(8):
                pic_out[0, 0, 8 * i + r, pl.ds(k, 1), :] = acc[k][r : r + 1, :]
        return carry

    lax.fori_loop(0, per_owner // 8, composite, 0)
    for d in order:
        to_mate(d).wait_send()
        onward(d).wait_send()
    pair_copy.wait_send()
    for face in [facesk, *faces1, *faces2, faces3]:
        face.wait_send()


def flush(state, picture, state_out, picture_out, sem):
    copies = [pltpu.make_async_copy(picture, picture_out, sem.at[NF])]
    copies += [pltpu.make_async_copy(state.at[f], state_out.at[f], sem.at[f]) for f in range(NF)]
    for copy in copies:
        copy.start()
    for copy in copies:
        copy.wait()


def shards(fields, diffusivity, courant, tf_center, tf_sharp, tf_gain, tf_color, tile_mask, tile_perm):
    nz = lax.axis_size("gz")
    per_owner = TILES // nz
    f32 = jnp.float32
    vm = pltpu.VMEM
    anywhere = pl.BlockSpec(memory_space=pl.ANY)
    inside = pl.BlockSpec(memory_space=pltpu.VMEM)

    def halo(n):
        return [vm((2, n, CZ, CX), f32), vm((2, n, CZ, CX), f32), vm((n, 8, CX), f32), vm((2, n, 8, CX), f32)]

    sm = lambda a: pltpu.SMEM(a.shape, a.dtype)
    operands = (
        fields, diffusivity, courant.T, tf_center, tf_sharp, tf_gain, tf_color,
        jnp.transpose(tile_mask, (0, 1, 3, 2)), tile_perm,
    )
    results = pl.pallas_call(
        kernel,
        out_shape=(vm((NF, CZ, CY, CX), f32), vm((1, 1, per_owner, 4, CX), f32)),
        in_specs=[anywhere] * 9,
        out_specs=(inside, inside),
        scratch_shapes=[
            vm((CZ + 2, 32, CX), f32),
            vm((NF, CZ + 2, 32, CX), f32),
            vm((NF, CZ + 2, 32, CX), f32),
            vm((CZ + 2, 32, CX), f32),
            *halo(1), *halo(NF), *halo(NF), *halo(1),
            vm((CZ + 1, CY, CX), f32),
            vm((5, CZ, CY, CX), f32),
            vm((CY, CZ, CX), f32),
            vm((CY, CZ, CX), f32),
            vm((CY, CZ, CX), f32),
            vm((3, CY, CZ, CX), f32),
            *[vm((max(nz // 2 - 1, 1), 4, per_owner, CX), f32)] * 3,
            *[vm((4, per_owner, CX), f32)] * 2,
            vm((nz // 2, 4, per_owner, CX), f32),
            *[sm(a) for a in operands[2:]],
            pltpu.SemaphoreType.DMA((72,)),
            pltpu.SemaphoreType.DMA((72,)),
            pltpu.SemaphoreType.DMA((nz,)),
            pltpu.SemaphoreType.DMA((nz,)),
            pltpu.SemaphoreType.DMA((13,)),
            pltpu.SemaphoreType.REGULAR((2,)),
        ],
        compiler_params=pltpu.CompilerParams(collective_id=0, has_side_effects=True),
        name="insitu",
    )(*operands)
    return pl.pallas_call(
        flush,
        out_shape=tuple(jax.ShapeDtypeStruct(r.shape, f32) for r in results),
        in_specs=[inside] * 2,
        out_specs=(anywhere, anywhere),
        scratch_shapes=[pltpu.SemaphoreType.DMA((NF + 1,))],
        name="flush",
    )(*[pltpu.with_memory_space_constraint(r, pltpu.VMEM) for r in results])


def solution(mesh):
    return jax.shard_map(
        shards,
        mesh=mesh,
        in_specs=(
            P(None, "gz", "gy", "gx"),
            P("gz", "gy", "gx"),
            P(),
            P(),
            P(),
            P(),
            P(),
            P("gz", None, "gy", "gx"),
            P("gy", "gx", None),
        ),
        out_specs=(P(None, "gz", "gy", "gx"), P("gy", "gx", "gz", None, None)),
        check_vma=False,
    )
```

```python
import functools
import math

import jax
import jax.numpy as jnp
from jax import lax
from jax.experimental import pallas as pl
from jax.experimental.pallas import tpu as pltpu
from jax.sharding import PartitionSpec as P

MESH = pl.DeviceIdType.MESH
LOG2E = math.log2(math.e)
NF, CZ, CY, CX, TF = 5, 32, 16, 128, 16
R0 = 8
TILES = TF * CY
GROUPS1 = ((0, 1), (1, 1), (2, 1), (3, 1), (4, 1))
GROUPS2 = ((0, 1), (1, 1), (2, 1), (3, 1), (4, 1))
UNROLL = 16


def kernel(
    fields, kappa, courant_in, center_in, sharp_in, gain_in, color_in, mask_in, perm_in,
    u2, pic_out,
    kb, u0, u1, sp, ysendk, yhalok, xsendk, xhalok, ysend1, yhalo1, xsend1, xhalo1,
    ysend2, yhalo2, xsend2, xhalo2, ysend3, yhalo3, xsend3, xhalo3,
    kz, kf, rs, rm, rh, rb, mtiles, mrecv, rtiles, ptiles, precv, recv,
    courant, center, sharp, gain, color, mask, perm,
    send_sem, recv_sem, tile_send, tile_recv, local_sem, token,
):
    f32 = jnp.float32
    names = ("gz", "gy", "gx")
    sizes = [lax.axis_size(a) for a in names]
    mes = [lax.axis_index(a) for a in names]
    nz = sizes[0]
    per_owner = TILES // nz
    rows = pl.ds(R0, CY)

    def exists(a, side):
        return (mes[a] > 0) if side == 0 else (mes[a] < sizes[a] - 1)

    ring = [lax.rem(mes[0] + 1, nz), lax.rem(mes[0] + nz - 1, nz)]
    barrier = pltpu.get_barrier_semaphore()

    def greet(sem):
        for z in ring:
            pl.semaphore_signal(sem, inc=1, device_id={"gz": z}, device_id_type=MESH)

    greet(barrier)
    count = jnp.int32(2)
    for a in (1, 2):
        for side in (0, 1):
            ok = exists(a, side)

            @pl.when(ok)
            def _(a=a, side=side):
                pl.semaphore_signal(
                    barrier, inc=1, device_id={names[a]: mes[a] + 2 * side - 1}, device_id_type=MESH
                )

            count = count + ok.astype(jnp.int32)

    def local(i, src, dst):
        copy = pltpu.make_async_copy(src, dst, local_sem.at[i])
        copy.start()
        return copy

    load_k = local(0, kappa, kb.at[pl.ds(1, CZ), rows, :])
    loads = [local(1 + f, fields.at[f], u0.at[f, pl.ds(1, CZ), rows, :]) for f in range(NF)]
    small = [
        local(6 + i, a, b)
        for i, (a, b) in enumerate(
            zip(
                (courant_in, center_in, sharp_in, gain_in, color_in, mask_in, perm_in),
                (courant, center, sharp, gain, color, mask, perm),
            )
        )
    ]

    lane = lax.broadcasted_iota(jnp.int32, (8, 128), 1)
    sub = lax.broadcasted_iota(jnp.int32, (8, 128), 0)
    pair = lax.bitwise_and(lax.shift_right_logical(lane + 1, 1), 63)
    even = lax.bitwise_and(lane, 1) == 0
    first_lane, last_lane = lane == 0, lane == CX - 1
    first_row, last_row = sub == 0, sub == 7
    blank = jnp.zeros((8, 128), f32)

    def rolled(x, shift):
        return pltpu.roll(x, shift, 1)

    def packed(value, into, v):
        return jnp.where(pair == v, rolled(value, 2 * v), into)

    def halo_pack(ref, f):
        return jnp.where(even, rolled(ref[0, f], 1), rolled(ref[1, f], CX - 1))

    for a, side, refs in (
        (0, 0, (kb.at[0, rows, :], u0.at[:, 0, rows, :], u1.at[:, 0, rows, :], sp.at[0, rows, :])),
        (0, 1, (kb.at[CZ + 1, rows, :], u0.at[:, CZ + 1, rows, :], u1.at[:, CZ + 1, rows, :], sp.at[CZ + 1, rows, :])),
        *((1, s, tuple(r.at[s] for r in (yhalok, yhalo1, yhalo2, yhalo3))) for s in (0, 1)),
        *((2, s, tuple(r.at[s] for r in (xhalok, xhalo1, xhalo2, xhalo3))) for s in (0, 1)),
    ):

        @pl.when(jnp.logical_not(exists(a, side)))
        def _(refs=refs):
            for r in refs:
                r[...] = jnp.zeros(r.shape, f32)

    class Faces:
        def __init__(self, sem, parts):
            self.sem, self.parts = sem, parts

        def desc(self, a, side):
            src, dst = self.parts[2 * a + side]
            i = self.sem + 2 * a + side
            return pltpu.make_async_remote_copy(
                src_ref=src, dst_ref=dst, send_sem=send_sem.at[i], recv_sem=recv_sem.at[i],
                device_id={names[a]: mes[a] + 2 * side - 1}, device_id_type=MESH,
            )

        def each(self, what, incoming):
            for a in (1, 2, 0):
                for side in (0, 1):

                    @pl.when(exists(a, 1 - side if incoming else side))
                    def _(a=a, side=side):
                        getattr(self.desc(a, side), what)()

        def start(self):
            self.each("start", False)

        def wait_recv(self):
            self.each("wait_recv", True)

        def wait_send(self):
            self.each("wait_send", False)

    def yx_parts(ys, yh, xs, xh, at):
        return [
            (ys.at[0, at], yh.at[1, at]), (ys.at[1, at], yh.at[0, at]),
            (xs.at[at], xh.at[1, at]), (xs.at[at], xh.at[0, at]),
        ]

    one = pl.ds(0, 1)
    facesk = Faces(0, [
        (kappa.at[0], kb.at[CZ + 1, rows, :]), (kappa.at[CZ - 1], kb.at[0, rows, :]),
        *yx_parts(ysendk, yhalok, xsendk, xhalok, one),
    ])
    faces1, faces2 = [], []
    for g, (f, n) in enumerate(GROUPS1):
        at = pl.ds(f, n)
        faces1.append(Faces(6 + 6 * g, [
            (fields.at[at, 0], u0.at[at, CZ + 1, rows, :]), (fields.at[at, CZ - 1], u0.at[at, 0, rows, :]),
            *yx_parts(ysend1, yhalo1, xsend1, xhalo1, at),
        ]))
    for g, (f, n) in enumerate(GROUPS2):
        at = pl.ds(f, n)
        faces2.append(Faces(36 + 6 * g, [
            (u1.at[at, 1, rows, :], u1.at[at, CZ + 1, rows, :]), (u1.at[at, CZ, rows, :], u1.at[at, 0, rows, :]),
            *yx_parts(ysend2, yhalo2, xsend2, xhalo2, at),
        ]))
    faces3 = Faces(66, [
        (sp.at[1, rows, :], sp.at[CZ + 1, rows, :]), (sp.at[CZ, rows, :], sp.at[0, rows, :]),
        *yx_parts(ysend3, yhalo3, xsend3, xhalo3, one),
    ])

    def sweep(body, init):
        def step(i, carry):
            for j in range(UNROLL):
                carry = body(UNROLL * i + j, carry)
            return carry

        return lax.fori_loop(0, CZ // UNROLL, step, init)

    def pack_planes(ref, ysend, xsend, f):
        def body(z, q):
            ysend[0, f, pl.ds(z, 1), :] = ref[z + 1, pl.ds(R0, 1), :]
            ysend[1, f, pl.ds(z, 1), :] = ref[z + 1, pl.ds(R0 + CY - 1, 1), :]
            for h in range(2):
                q = packed(ref[z + 1, pl.ds(R0 + 8 * h, 8), :], q, 2 * z + h)
            return q

        xsend[f] = sweep(body, blank)

    load_k.wait()
    pack_planes(kb, ysendk, xsendk, 0)
    pl.semaphore_wait(barrier, count)
    facesk.start()
    for f in range(NF):
        loads[f].wait()
        pack_planes(u0.at[f], ysend1, xsend1, f)
        for g, (f0, n) in enumerate(GROUPS1):
            if f == f0 + n - 1:
                faces1[g].start()
    for copy in small:
        copy.wait()
    greet(token.at[0])

    def sides(ref, z, h, yhalo, f, pack):
        row = R0 + 8 * h
        mid = ref[z + 1, pl.ds(row, 8), :]
        zm, zp = ref[z, pl.ds(row, 8), :], ref[z + 2, pl.ds(row, 8), :]
        ym, yp = ref[z + 1, pl.ds(row - 1, 8), :], ref[z + 1, pl.ds(row + 1, 8), :]
        if h == 0:
            ym = jnp.where(first_row, jnp.broadcast_to(yhalo[0, f, pl.ds(z, 1), :], (8, 128)), ym)
        else:
            yp = jnp.where(last_row, jnp.broadcast_to(yhalo[1, f, pl.ds(z, 1), :], (8, 128)), yp)
        edge = rolled(pack, lax.rem(128 - 2 * (2 * z + h), 128))
        xm = jnp.where(first_lane, edge, rolled(mid, 1))
        xp = jnp.where(last_lane, edge, rolled(mid, CX - 1))
        return mid, zm, zp, ym, yp, xm, xp

    facesk.wait_recv()
    kpack = halo_pack(xhalok, 0)

    def coefficients(z, carry):
        for h in range(2):
            at = pl.ds(8 * h, 8)
            mid, *others = sides(kb, z, h, yhalok, 0, kpack)
            means = [0.5 * (mid + w) for w in others]
            kz[z, at, :] = means[0]
            kz[z + 1, at, :] = means[1]
            for i in range(4):
                kf[i, z, at, :] = means[2 + i]
            kf[4, z, at, :] = 1.0 - ((means[0] + means[1]) + (means[2] + means[3]) + (means[4] + means[5]))
        return carry

    sweep(coefficients, 0)

    def advance(src, f, yhalo, xhalo, emit):
        pack = halo_pack(xhalo, f)
        cz, cy, cx = courant[0, f], courant[1, f], courant[2, f]
        total = cz + cy + cx

        def body(z, q):
            for h in range(2):
                at = pl.ds(8 * h, 8)
                mid, zm, zp, ym, yp, xm, xp = sides(src.at[f], z, h, yhalo, f, pack)
                value = (
                    (kf[4, z, at, :] - total) * mid
                    + (kz[z + 1, at, :] * zp + (kz[z, at, :] + cz) * zm)
                    + (kf[1, z, at, :] * yp + (kf[0, z, at, :] + cy) * ym)
                    + (kf[3, z, at, :] * xp + (kf[2, z, at, :] + cx) * xm)
                )
                emit(z, h, value)
                if q is not None:
                    q = packed(value, q, 2 * z + h)
            return q

        return body

    def step1(f):
        def emit(z, h, value):
            u1[f, z + 1, pl.ds(R0 + 8 * h, 8), :] = value
            side, row = (0, 0) if h == 0 else (1, 7)
            ysend2[side, f, pl.ds(z, 1), :] = value[row : row + 1, :]

        xsend2[f] = sweep(advance(u0, f, yhalo1, xhalo1, emit), blank)

    arrivals1 = {f: faces1[g] for g, (f, n) in enumerate(GROUPS1)}
    departures2 = {f + n - 1: faces2[g] for g, (f, n) in enumerate(GROUPS2)}
    for f in range(NF):
        if f in arrivals1:
            arrivals1[f].wait_recv()
        step1(f)
        if f in departures2:
            departures2[f].start()
    pl.semaphore_wait(token.at[0], 2)
    greet(token.at[1])

    def sites(z, h):
        start = h * 8 * CZ + lax.rem(z, 4) * 8 + lax.div(z, 4)
        return pl.ds(start, 8, stride=CZ)

    rs2, rm2 = rs.reshape(CY * CZ, CX), rm.reshape(CY * CZ, CX)
    rh2, rb2 = rh.reshape(CY * CZ, CX), rb.reshape(3, CY * CZ, CX)

    def step2(f):
        def emit(z, h, value):
            at = pl.ds(8 * h, 8)
            u2[f, z, at, :] = value
            if f == 0:
                sp[z + 1, pl.ds(R0 + 8 * h, 8), :] = value
                side, row = (0, 0) if h == 0 else (1, 7)
                ysend3[side, 0, pl.ds(z, 1), :] = value[row : row + 1, :]
                rs2[sites(z, h), :] = value
            elif f == 4:
                rm2[sites(z, h), :] = (-LOG2E) - (0.5 * LOG2E) * jnp.tanh(value)
            else:
                rb2[f - 1, sites(z, h), :] = 0.5 + 0.5 * jnp.tanh(0.5 * value)

        out = sweep(advance(u1, f, yhalo2, xhalo2, emit), blank if f == 0 else None)
        if f == 0:
            xsend3[0] = out

    arrivals2 = {f: faces2[g] for g, (f, n) in enumerate(GROUPS2)}
    for f in range(NF):
        if f in arrivals2:
            arrivals2[f].wait_recv()
        step2(f)
        if f == 0:
            faces3.start()

    faces3.wait_recv()
    spack = halo_pack(xhalo3, 0)

    def shading(z, carry):
        for h in range(2):
            _, zm, zp, ym, yp, xm, xp = sides(sp, z, h, yhalo3, 0, spack)
            gz, gy, gx = 0.5 * (zp - zm), 0.5 * (yp - ym), 0.5 * (xp - xm)
            shade = 0.35 + 0.65 * jnp.abs(0.64 * gz + 0.6 * gy + 0.48 * gx) * lax.rsqrt(
                gz * gz + gy * gy + gx * gx + 1.0
            )
            rh2[sites(z, h), :] = shade
        return carry

    sweep(shading, 0)
    pl.semaphore_wait(token.at[1], 2)

    pairs, relays = nz // 2, nz // 2 - 1
    odd = lax.rem(mes[0], 2)
    ahead = 2 * odd - 1
    mate = mes[0] - ahead
    mine = lax.div(mes[0], 2)

    def at_distance(start, d):
        return lax.rem(start + d * ahead + nz, nz)

    def block_copy(i, src, dst, z):
        return pltpu.make_async_remote_copy(
            src_ref=src, dst_ref=dst, send_sem=tile_send.at[i], recv_sem=tile_recv.at[i],
            device_id={"gz": z}, device_id_type=MESH,
        )

    def render(owner, dst):
        def tile(i, carry):
            p = perm[0, 0, owner * per_owner + i]
            t = lax.shift_right_logical(p, 4)
            y = lax.bitwise_and(p, 15)
            cover = mask[0, t, 0, y].astype(f32)
            mid, slope, amount = center[t], -LOG2E * sharp[t], gain[t]
            gap = rs[y] - mid
            depth = jnp.exp2(slope * (gap * gap)) * (amount * rm[y])
            e = [depth[0:8]]
            for w in range(1, 4):
                e.append(e[-1] + depth[8 * w : 8 * w + 8])
            inclusive = e[3]
            for sh in (1, 2, 4):
                inclusive = inclusive + jnp.where(sub >= sh, pltpu.roll(inclusive, sh, 0), 0.0)
            before = jnp.exp2(inclusive - e[3])
            lit = [jnp.exp2(x) for x in e]
            weight = [1.0 - lit[0]] + [lit[w] - lit[w + 1] for w in range(3)]
            shade = rh[y]
            weight = [weight[w] * shade[8 * w : 8 * w + 8] for w in range(4)]
            for k in range(3):
                base = rb[k, y]
                total = weight[0] * base[0:8]
                for w in range(1, 4):
                    total = total + weight[w] * base[8 * w : 8 * w + 8]
                total = jnp.sum(total * before, axis=0, keepdims=True)
                dst[k, pl.ds(i, 1), :] = total * (color[k, t] * cover)
            dst[3, pl.ds(i, 1), :] = (1.0 - jnp.exp2(inclusive[7:8])) * cover
            return carry

        lax.fori_loop(0, per_owner, tile, 0, unroll=4)

    def merge(theirs, own):
        for i in range(per_owner // 8):
            at = pl.ds(8 * i, 8)
            a = [theirs[k, at, :] for k in range(4)]
            b = [own[k, at, :] for k in range(4)]
            front = [jnp.where(odd == 1, x, y) for x, y in zip(a, b)]
            back = [jnp.where(odd == 1, y, x) for x, y in zip(a, b)]
            clear = 1.0 - front[3]
            for k in range(4):
                own[k, at, :] = front[k] + clear * back[k]

    def to_mate(d):
        return block_copy(pairs + d, mtiles.at[d - 1], mrecv.at[d - 1], mate)

    def onward(d):
        return pltpu.make_async_remote_copy(
            src_ref=rtiles.at[d - 1], dst_ref=recv.at[mine],
            send_sem=tile_send.at[d - 1], recv_sem=tile_recv.at[mine],
            device_id={"gz": at_distance(mes[0], d)}, device_id_type=MESH,
        )

    def pass_on(d):
        to_mate(d).wait_recv()
        merge(mrecv.at[d - 1], rtiles.at[d - 1])
        onward(d).start()

    order = list(range(relays, 0, -1))
    for d in order:
        render(at_distance(mate, -d), mtiles.at[d - 1])
        to_mate(d).start()
    pair_copy = block_copy(pairs, ptiles, precv, mate)
    for j, d in enumerate(order):
        render(at_distance(mes[0], d), rtiles.at[d - 1])
        if j:
            pass_on(order[j - 1])
    render(mate, ptiles)
    pair_copy.start()
    if order:
        pass_on(order[-1])
    render(mes[0], recv.at[mine])
    pair_copy.wait_recv()
    merge(precv, recv.at[mine])
    for o in range(1, pairs):
        q = lax.rem(mine + o, pairs)
        pltpu.make_async_remote_copy(
            src_ref=rtiles.at[0], dst_ref=recv.at[q], send_sem=tile_send.at[0], recv_sem=tile_recv.at[q],
            device_id={"gz": mate}, device_id_type=MESH,
        ).wait_recv()

    def composite(i, carry):
        at = pl.ds(pl.multiple_of(8 * i, 8), 8)
        acc = [recv[0, k, at, :] for k in range(4)]
        for s in range(1, pairs):
            clear = 1.0 - acc[3]
            acc = [acc[k] + clear * recv[s, k, at, :] for k in range(4)]
        for k in range(4):
            for r in range(8):
                pic_out[0, 0, 8 * i + r, pl.ds(k, 1), :] = acc[k][r : r + 1, :]
        return carry

    lax.fori_loop(0, per_owner // 8, composite, 0)
    for d in order:
        to_mate(d).wait_send()
        onward(d).wait_send()
    pair_copy.wait_send()
    for face in [facesk, *faces1, *faces2, faces3]:
        face.wait_send()


def flush(state, picture, state_out, picture_out, sem):
    copies = [pltpu.make_async_copy(picture, picture_out, sem.at[NF])]
    copies += [pltpu.make_async_copy(state.at[f], state_out.at[f], sem.at[f]) for f in range(NF)]
    for copy in copies:
        copy.start()
    for copy in copies:
        copy.wait()


def shards(fields, diffusivity, courant, tf_center, tf_sharp, tf_gain, tf_color, tile_mask, tile_perm):
    nz = lax.axis_size("gz")
    per_owner = TILES // nz
    f32 = jnp.float32
    vm = pltpu.VMEM
    anywhere = pl.BlockSpec(memory_space=pl.ANY)
    inside = pl.BlockSpec(memory_space=pltpu.VMEM)

    def halo(n):
        return [vm((2, n, CZ, CX), f32), vm((2, n, CZ, CX), f32), vm((n, 8, CX), f32), vm((2, n, 8, CX), f32)]

    sm = lambda a: pltpu.SMEM(a.shape, a.dtype)
    operands = (
        fields, diffusivity, courant.T, tf_center, tf_sharp, tf_gain, tf_color,
        jnp.transpose(tile_mask, (0, 1, 3, 2)), tile_perm,
    )
    results = pl.pallas_call(
        kernel,
        out_shape=(vm((NF, CZ, CY, CX), f32), vm((1, 1, per_owner, 4, CX), f32)),
        in_specs=[anywhere] * 9,
        out_specs=(inside, inside),
        scratch_shapes=[
            vm((CZ + 2, 32, CX), f32),
            vm((NF, CZ + 2, 32, CX), f32),
            vm((NF, CZ + 2, 32, CX), f32),
            vm((CZ + 2, 32, CX), f32),
            *halo(1), *halo(NF), *halo(NF), *halo(1),
            vm((CZ + 1, CY, CX), f32),
            vm((5, CZ, CY, CX), f32),
            vm((CY, CZ, CX), f32),
            vm((CY, CZ, CX), f32),
            vm((CY, CZ, CX), f32),
            vm((3, CY, CZ, CX), f32),
            *[vm((max(nz // 2 - 1, 1), 4, per_owner, CX), f32)] * 3,
            *[vm((4, per_owner, CX), f32)] * 2,
            vm((nz // 2, 4, per_owner, CX), f32),
            *[sm(a) for a in operands[2:]],
            pltpu.SemaphoreType.DMA((72,)),
            pltpu.SemaphoreType.DMA((72,)),
            pltpu.SemaphoreType.DMA((nz,)),
            pltpu.SemaphoreType.DMA((nz,)),
            pltpu.SemaphoreType.DMA((13,)),
            pltpu.SemaphoreType.REGULAR((2,)),
        ],
        compiler_params=pltpu.CompilerParams(collective_id=0, has_side_effects=True),
        name="insitu",
    )(*operands)
    return pl.pallas_call(
        flush,
        out_shape=tuple(jax.ShapeDtypeStruct(r.shape, f32) for r in results),
        in_specs=[inside] * 2,
        out_specs=(anywhere, anywhere),
        scratch_shapes=[pltpu.SemaphoreType.DMA((NF + 1,))],
        name="flush",
    )(*[pltpu.with_memory_space_constraint(r, pltpu.VMEM) for r in results])


def solution(mesh):
    return jax.shard_map(
        shards,
        mesh=mesh,
        in_specs=(
            P(None, "gz", "gy", "gx"),
            P("gz", "gy", "gx"),
            P(),
            P(),
            P(),
            P(),
            P(),
            P("gz", None, "gy", "gx"),
            P("gy", "gx", None),
        ),
        out_specs=(P(None, "gz", "gy", "gx"), P("gy", "gx", "gz", None, None)),
        check_vma=False,
    )
```
